32 devices in a mesh: groups: 2 (over x), slab: 16 (over z, y, core).
Axes of the slice: x: 2, y: 2, z: 4, core: 2. Of those that a mesh axis runs over, the one named last changes fastest.
Arguments:
- recorded: float32 [3, 256, 256, 128], P(None, 'slab', 'groups'), parts along dimension 2, may hold values from 0.02 to 14, as said below
- initial: float32 [256, 256, 128], P('slab', 'groups'), parts along dimension 1, may hold values from 0.5 to 2
- kernel_x: float32 [3, 64], replicated, may hold values from 0.01 to 1.05, as said below
- kernel_y: float32 [3, 64], replicated, may hold values from 0.01 to 1.05, as said below
- kernel_z: float32 [3, 32], replicated, may hold values from 0.01 to 1.05, as said below
Outputs:
- deconvolved: float32 [256, 256, 128], P('slab', 'groups'), parts along dimension 1
The draws below stay inside these ranges and needn't reach their ends.
There are 2 independent parts, one for each index of `groups`. The reference program is written for one: setup_inputs(seed, part) draws one part's arguments, and reference() takes and returns one part's arrays. A program takes and returns all parts, laid end to end along the dimension named above; an argument that names none is the same for every part. Nothing has to cross between parts.
Inputs may be any that keep to these rules, and one draw needn't show every extreme that they name: `recorded`: positive intensities. `kernel_x`: positive taps. `kernel_y`: positive taps. `kernel_z`: positive taps.
All inputs are finite; a program needn't handle non-finite values.
Results may differ from the reference program's by a relative error of at most 0.0001.
Values sent between devices are 32-bit elements; how exact they have to be, the bound alone decides.
No kernel may reach another device: no remote copies, remote signals or barrier semaphores. Data moves between devices by JAX's collectives and lax.ppermute only.
A program may use at most 128 MiB of HBM per device.

```python
import math
import jax
import jax.numpy as jnp
from jax import lax

LX = 128
LY = 128
KL = 64
KZ = 32
V = 3
CZ = 16
ITERS = 2
H = 16
Z = 256


def peaked_taps(key, fwhm, taps):
    sigma = fwhm / 2.3548
    offsets = jnp.arange(taps, dtype=jnp.float32) - float(taps // 2)
    peak = jnp.exp(-0.5 * (offsets[None, :] / sigma[:, None]) ** 2)
    floor = jax.random.uniform(key, (fwhm.shape[0], taps), jnp.float32, 0.01, 0.05)
    return peak + floor


def pick_widths(key, low_width, high_width):
    widths = jnp.exp(jax.random.uniform(key, (V,), jnp.float32, math.log(low_width), math.log(high_width)))
    return widths


def draw_kernel_x(key, part):
    width_key, floor_key = jax.random.split(jax.random.fold_in(key, 11))
    return peaked_taps(floor_key, pick_widths(width_key, 2.0, 6.0), KL)


def draw_kernel_y(key, part):
    width_key, floor_key = jax.random.split(jax.random.fold_in(key, 23))
    return peaked_taps(floor_key, pick_widths(width_key, 2.0, 6.0), KL)


def draw_kernel_z(key, part):
    width_key, floor_key = jax.random.split(jax.random.fold_in(key, 37))
    return peaked_taps(floor_key, pick_widths(width_key, 6.0, 16.0), KZ)


def draw_recorded(key, part):
    noise_key = jax.random.fold_in(key, 0)
    bead_key = jax.random.fold_in(key, 3)
    bright_key = jax.random.fold_in(key, 4)
    depth_frac = jnp.arange(Z, dtype=jnp.float32) / (Z - 1)
    view_signs = jnp.where(jnp.arange(V) % 2 == 0, 1.0, -1.0).astype(jnp.float32)
    centred = view_signs[:, None] * (depth_frac[None, :] - 0.5) + 0.5
    profile = jnp.exp(math.log(3.0) * centred)
    noise_vals = jax.random.uniform(noise_key, (V, Z, LX, LY), jnp.float32, 0.5, 1.5)
    beads = jax.random.bernoulli(bead_key, 0.0625, (V, Z, LX, LY))
    brightness = jax.random.uniform(bright_key, (V, Z, LX, LY), jnp.float32, 1.0, 3.0)
    bead_factor = jnp.where(beads, brightness, 1.0)
    result_field = profile[:, :, None, None] * noise_vals * bead_factor
    return result_field


def block_levels(key, dims, cuts, low, high):
    factor_of = 1.0
    for axis_at, shards_of in cuts:
        draws = jax.random.uniform(jax.random.fold_in(jax.random.fold_in(key, 6), axis_at), (shards_of,), jnp.float32, low / len(cuts), high / len(cuts))
        factor_of = factor_of * jnp.repeat(jnp.exp(draws), dims[axis_at] // shards_of).reshape((-1,) + (1,) * (len(dims) - 1 - axis_at))
    return factor_of


def setup_inputs(seed: int = 0, part: int = 0) -> dict:
    keys = jax.random.split(jax.random.key(seed), 6)
    part_keys = jax.random.split(jax.random.fold_in(keys[5], part), 6)
    recorded = draw_recorded(jax.random.fold_in(jax.random.fold_in(keys[5], part), 71), part)
    initial = jnp.clip(jnp.exp(math.log(2.0) - 1.3862944 * jax.random.uniform(part_keys[1], (Z, LX, LY), jnp.float32) ** block_levels(part_keys[1], (Z, LX, LY), ((0, 16),), -0.2, 0.2)), 0.5, 2.0)
    kernel_x = draw_kernel_x(jax.random.fold_in(keys[5], 71), part)
    kernel_y = draw_kernel_y(jax.random.fold_in(keys[5], 71), part)
    kernel_z = draw_kernel_z(jax.random.fold_in(keys[5], 71), part)
    return dict(recorded=recorded, initial=initial, kernel_x=kernel_x, kernel_y=kernel_y, kernel_z=kernel_z)


PRECISE = lax.Precision.HIGHEST


def normalize(kernel):
    kernel = kernel.astype(jnp.float32)
    return kernel / jnp.sum(kernel, axis=1, keepdims=True)


def lateral_matrix(kernel, length):
    tap_count = kernel.shape[1]
    row_ids = jnp.arange(length)[:, None, None]
    col_ids = jnp.arange(length)[None, :, None]
    tap_ids = jnp.arange(tap_count)[None, None, :]
    pick_table = (col_ids - row_ids + tap_count // 2 == tap_ids).astype(jnp.float32)
    return jnp.einsum("ijk,vk->vij", pick_table, kernel, precision=PRECISE)


def axial_bands(kernel, block_len, reach_len):
    tap_count = kernel.shape[1]
    row_ids = jnp.arange(block_len)[:, None, None]
    col_ids = jnp.arange(block_len + 2 * reach_len)[None, :, None]
    tap_ids = jnp.arange(tap_count)[None, None, :]
    ahead_pick = (col_ids - row_ids == tap_ids).astype(jnp.float32)
    behind_pick = (row_ids - col_ids + 2 * reach_len == tap_ids).astype(jnp.float32)
    forward = jnp.einsum("ijk,vk->vij", ahead_pick, kernel, precision=PRECISE)
    backward = jnp.einsum("ijk,vk->vij", behind_pick, kernel, precision=PRECISE)
    return forward, backward


def axial_apply(field, bands):
    padded = jnp.pad(field, ((H, H), (0, 0), (0, 0)))
    flattened = padded.reshape(padded.shape[0], -1)

    def one_block(block_id):
        window = lax.dynamic_slice_in_dim(flattened, block_id * CZ, CZ + 2 * H, 0)
        return jnp.dot(bands, window, precision=PRECISE, preferred_element_type=jnp.float32)

    stacked = lax.map(one_block, jnp.arange(Z // CZ, dtype=jnp.int32))
    return stacked.reshape(field.shape)


def reference(recorded, initial, kernel_x, kernel_y, kernel_z):
    norm_x = normalize(kernel_x)
    norm_y = normalize(kernel_y)
    norm_z = normalize(kernel_z)
    mat_x = lateral_matrix(norm_x, LX)
    mat_y = lateral_matrix(norm_y, LY)
    ahead_bands, behind_bands = axial_bands(norm_z, CZ, H)
    measured = recorded.astype(jnp.float32)
    estimate = initial.astype(jnp.float32)
    view_gains = []
    for iteration in range(ITERS):
        correction = jnp.zeros_like(estimate)
        for view_id in range(V):
            axial_blur = axial_apply(estimate, ahead_bands[view_id])
            along_x = jnp.einsum("ix,zxy->ziy", mat_x[view_id], axial_blur, precision=PRECISE)
            blurred = jnp.einsum("jy,ziy->zij", mat_y[view_id], along_x, precision=PRECISE)
            if iteration == 0:
                view_gains.append(jnp.sum(blurred) / jnp.sum(measured[view_id]))
            quotient = view_gains[view_id] * measured[view_id] / blurred
            back_y = jnp.einsum("jy,zij->ziy", mat_y[view_id], quotient, precision=PRECISE)
            back_x = jnp.einsum("ix,ziy->zxy", mat_x[view_id], back_y, precision=PRECISE)
            correction = correction + axial_apply(back_x, behind_bands[view_id])
        estimate = estimate * correction / V
    return estimate
```

```python
import functools

import jax
import jax.numpy as jnp
from jax import lax
from jax.experimental import pallas as pl
from jax.experimental.pallas import tpu as pltpu
from jax.sharding import PartitionSpec as P

ITERS = 2
CHUNKS = 2
GROUP = 8
LANES = 128
F32 = jnp.float32
BF16 = jnp.bfloat16
PRECISE = lax.Precision.HIGHEST


def split(value):
    high = value.astype(BF16)
    low = (value - high.astype(F32)).astype(BF16)
    return high, low


def dot(left, right):
    return jnp.dot(left, right, preferred_element_type=F32)


def normalize(kernel):
    return kernel / jnp.sum(kernel, axis=1, keepdims=True)


def lateral_kernel(taps_x, taps_y, fwd_x, bwd_x, fwd_y, bwd_y, sums_x, sums_y, *, tap_count):
    view_count = taps_x.shape[0]
    size = fwd_x.shape[1]
    rows = lax.broadcasted_iota(jnp.int32, (size, size), 0)
    cols = lax.broadcasted_iota(jnp.int32, (size, size), 1)
    tap_ids = cols - rows + tap_count // 2
    inside = (tap_ids >= 0) & (tap_ids < tap_count)
    for taps, is_x in ((taps_x, True), (taps_y, False)):
        values = taps[...]
        values = values / jnp.sum(values, axis=1, keepdims=True)
        for view in range(view_count):
            line = jnp.broadcast_to(values[view : view + 1, :], (size, size))
            matrix = pltpu.roll(line, size - tap_count // 2, 1, stride=1, stride_axis=0)
            matrix = jnp.where(inside, matrix, 0.0)
            high, low = split(matrix)
            high_t, low_t = split(matrix.T)
            total = jnp.sum(matrix, axis=0, keepdims=True)
            if is_x:
                fwd_x[view] = jnp.concatenate([high, high, low], axis=1)
                bwd_x[view] = jnp.concatenate([high_t, high_t, low_t], axis=1)
                sums_x[view : view + 1, :] = total
            else:
                one = jnp.concatenate([high_t, low_t], axis=1)
                fwd_y[view] = jnp.concatenate([one, one], axis=0)
                one = jnp.concatenate([high, low], axis=1)
                bwd_y[view] = jnp.concatenate([one, one], axis=0)
                sums_y[view : view + 1, :] = total


def lateral_matrices(kernel_x, kernel_y, size_x, size_y):
    view_count, tap_count = kernel_x.shape
    assert size_x == size_y == LANES and tap_count <= size_x
    pads = ((0, 0), (0, size_x - tap_count))
    out = lambda *shape: jax.ShapeDtypeStruct(shape, BF16)
    return pl.pallas_call(
        functools.partial(lateral_kernel, tap_count=tap_count),
        out_shape=(
            out(view_count, size_x, 3 * size_x),
            out(view_count, size_x, 3 * size_x),
            out(view_count, 2 * size_y, 2 * size_y),
            out(view_count, 2 * size_y, 2 * size_y),
            jax.ShapeDtypeStruct((view_count, size_x), F32),
            jax.ShapeDtypeStruct((view_count, size_y), F32),
        ),
        name="lateral_matrices",
    )(jnp.pad(kernel_x, pads), jnp.pad(kernel_y, pads))


def axial_matrices(taps, block_len, odd):
    view_count, tap_count = taps.shape
    reach = tap_count // 2
    base = jnp.arange(block_len)
    near = jnp.where(odd, -block_len, block_len)
    source = jnp.concatenate([base, base + near, base - near])
    tap_ids = source[None, :] - base[:, None] + reach
    pick = (tap_ids[:, :, None] == jnp.arange(tap_count)).astype(F32)
    bands = jnp.einsum("zsk,vk->vzs", pick, taps, precision=PRECISE)
    return bands.reshape(view_count * block_len, -1)


def stacked(matrix):
    high = lax.reduce_precision(matrix, 8, 7)
    low = matrix - high
    return jnp.concatenate([high, high, low], axis=1).astype(BF16)


def totals_kernel(recorded, initial, sums_x, sums_y, weights_z, out, *, block_len):
    view_count = sums_x.shape[0]
    lanes = lax.broadcasted_iota(jnp.int32, out.shape, 1)
    view_of = (lanes % (view_count * block_len)) // block_len
    row_of = lax.broadcasted_iota(jnp.int32, out.shape, 0)
    along_x = sums_x[...]
    weighted = jnp.zeros(sums_y.shape, F32)
    for z in range(block_len):
        part = jnp.dot(along_x, initial[z], precision=PRECISE, preferred_element_type=F32)
        weighted = weighted + part * weights_z[:, z : z + 1]
    weighted = weighted * sums_y[...]
    result = jnp.zeros(out.shape, F32)
    for view in range(view_count):

        def add(z, total):
            return total + jnp.sum(recorded[view * block_len + z].reshape(-1, 8, LANES), axis=0)

        data = lax.fori_loop(0, block_len, add, jnp.zeros((8, LANES), F32), unroll=4)
        blur_total = jnp.sum(weighted[view : view + 1, :])
        data_total = jnp.sum(data)
        value = jnp.where(row_of == 0, data_total, blur_total)
        result = jnp.where(view_of == view, value, result)
    out[...] = result


def totals(recorded, initial, sums_x, sums_y, taps, axis):
    block_len = initial.shape[0]
    view_count, tap_count = taps.shape
    count = lax.axis_size(axis)
    plane = lax.axis_index(axis) * block_len + jnp.arange(block_len)
    target = plane[:, None] + tap_count // 2 - jnp.arange(tap_count)[None, :]
    inside = ((target >= 0) & (target < count * block_len)).astype(F32)
    weights = jnp.sum(taps[:, None, :] * inside[None], axis=2)
    mine = pl.pallas_call(
        functools.partial(totals_kernel, block_len=block_len),
        out_shape=jax.ShapeDtypeStruct((8, 2 * LANES), F32),
        name="totals",
    )(recorded, initial, sums_x, sums_y, weights)
    copies = jnp.broadcast_to(mine[None], (count,) + mine.shape)
    return lax.all_to_all(copies, axis, 0, 0)


def forward_kernel(own, near, far, axial, lateral, out, *, block_len):
    chunk = own.shape[0]
    view_count = lateral.shape[0]
    axial_matrix = axial[...]

    def step(index, carry):
        start = index * GROUP
        window = jnp.concatenate(
            [ref[pl.ds(start, GROUP)] for ref in (own, near, far)], axis=1
        )
        high, low = split(window)
        terms = jnp.concatenate([high, low, high], axis=1)
        blurred = []
        for pair in range(0, GROUP, 2):
            blurred.append(dot(axial_matrix, jnp.concatenate([terms[pair], terms[pair + 1]], axis=1)))
        for view in range(view_count):
            rows = slice(view * block_len, (view + 1) * block_len)
            field = jnp.concatenate(
                [part[rows, side : side + LANES] for part in blurred for side in (0, LANES)], axis=0
            )
            result = dot(jnp.concatenate(split(field), axis=1), lateral[view])
            result = result[:, :LANES] + result[:, LANES:]
            for i in range(GROUP):
                first = view * block_len * chunk + start + i
                out[pl.ds(first, block_len, stride=chunk), :] = result[
                    i * block_len : (i + 1) * block_len
                ]
        return carry

    lax.fori_loop(0, chunk // GROUP, step, 0)


def forward_part(own, near, far, axial, lateral):
    chunk, block_len, size_y = own.shape
    view_count = lateral.shape[0]
    return pl.pallas_call(
        functools.partial(forward_kernel, block_len=block_len),
        out_shape=jax.ShapeDtypeStruct((view_count * block_len * chunk, size_y), F32),
        name="forward_part",
    )(own, near, far, axial, lateral)


def quotient_kernel(*refs, chunks, block_len):
    parts, (recorded, fwd, bwd, out) = refs[:chunks], refs[chunks:]
    view_count = fwd.shape[0]
    chunk = parts[0].shape[0] // (view_count * block_len)
    planes = view_count * block_len
    size_x = chunk * chunks
    for view in range(view_count):

        def step(index, carry):
            plane = view * block_len + 2 * index
            field = jnp.concatenate(
                [
                    jnp.concatenate([ref[pl.ds((plane + side) * chunk, chunk), :] for ref in parts], axis=0)
                    for side in (0, 1)
                ],
                axis=1,
            )
            high, low = split(field)
            blurred = dot(fwd[view], jnp.concatenate([high, low, high], axis=0))
            data = jnp.concatenate([recorded[plane], recorded[plane + 1]], axis=1)
            high, low = split(data / blurred)
            back = dot(bwd[view], jnp.concatenate([high, low, high], axis=0))
            out[pl.ds(plane, size_x, stride=planes), :] = back[:, :LANES]
            out[pl.ds(plane + 1, size_x, stride=planes), :] = back[:, LANES:]
            return carry

        lax.fori_loop(0, block_len // 2, step, 0, unroll=2)


def quotient_part(parts, recorded, fwd, bwd):
    planes, size_x, size_y = recorded.shape
    view_count = fwd.shape[0]
    return pl.pallas_call(
        functools.partial(quotient_kernel, chunks=len(parts), block_len=planes // view_count),
        out_shape=jax.ShapeDtypeStruct((size_x * planes, size_y), F32),
        name="quotient_part",
    )(*parts, recorded, fwd, bwd)


def backward_kernel(field, axial, sums, lateral, own, near, far, *, block_len, offset):
    chunk = own.shape[0]
    view_count = lateral.shape[0]
    planes = view_count * block_len
    total = jnp.sum(sums[...], axis=0)
    gains = (total[1:2, :] / total[0:1, :])[:, : axial.shape[1]]
    scaled = axial[...] * gains
    high, low = split(scaled)
    lanes = lax.broadcasted_iota(jnp.int32, scaled.shape, 1)
    axial_matrix = jnp.where(lanes < 2 * planes, high.astype(F32), low.astype(F32)).astype(BF16)

    def step(index, carry):
        start = index * GROUP
        rows = field[pl.ds((offset + start) * planes, GROUP * planes), :].reshape(GROUP, planes, LANES)
        results = []
        for view in range(view_count):
            part = rows[:, view * block_len : (view + 1) * block_len, :].reshape(GROUP * block_len, LANES)
            result = dot(jnp.concatenate(split(part), axis=1), lateral[view])
            results.append((result[:, :LANES] + result[:, LANES:]).reshape(GROUP, block_len, LANES))
        high, low = split(jnp.concatenate(results, axis=1))
        terms = jnp.concatenate([high, low, high], axis=1)
        for pair in range(0, GROUP, 2):
            sent = dot(axial_matrix, jnp.concatenate([terms[pair], terms[pair + 1]], axis=1))
            for side in (0, 1):
                lanes_of = slice(side * LANES, (side + 1) * LANES)
                for place, ref in enumerate((own, near, far)):
                    ref[start + pair + side] = sent[place * block_len : (place + 1) * block_len, lanes_of]
        return carry

    lax.fori_loop(0, chunk // GROUP, step, 0)


def backward_part(field, axial, sums, lateral, block_len, chunk, offset):
    size_y = field.shape[1]
    shape = jax.ShapeDtypeStruct((chunk, block_len, size_y), F32)
    return pl.pallas_call(
        functools.partial(backward_kernel, block_len=block_len, offset=offset),
        out_shape=(shape, shape, shape),
        name="backward_part",
    )(field, axial, sums, lateral)


def body(recorded, initial, kernel_x, kernel_y, kernel_z):
    view_count, block_len, size_x, size_y = recorded.shape
    assert kernel_z.shape[1] // 2 <= block_len
    count = lax.axis_size("slab")
    chunk = size_x // CHUNKS
    odd = lax.axis_index("slab") % 2 == 1
    near_pairs = [p for i in range(0, count - 1, 2) for p in ((i, i + 1), (i + 1, i))]
    far_pairs = [p for i in range(1, count - 1, 2) for p in ((i, i + 1), (i + 1, i))]

    def exchange(far_value, near_value):
        return lax.ppermute(far_value, "slab", far_pairs), lax.ppermute(near_value, "slab", near_pairs)

    turned = jnp.transpose(initial, (1, 0, 2))
    estimate = [turned[i * chunk : (i + 1) * chunk] for i in range(CHUNKS)]
    planes = recorded.reshape(view_count * block_len, size_x, size_y)
    fwd_x, bwd_x, fwd_y, bwd_y, sums_x, sums_y = lateral_matrices(kernel_x, kernel_y, size_x, size_y)
    taps_z = normalize(kernel_z)
    bands = axial_matrices(taps_z, block_len, odd)
    axial_fwd = stacked(bands)
    axial_bwd = jnp.concatenate([bands.T] * 3, axis=1)
    sums = totals(planes, initial, sums_x, sums_y, taps_z, "slab")
    for _ in range(ITERS):
        halos = [exchange(part, part) for part in estimate]
        parts = [
            forward_part(part, near, far, axial_fwd, fwd_y)
            for part, (far, near) in zip(estimate, halos)
        ]
        field = quotient_part(parts, planes, fwd_x, bwd_x)
        sent = [
            backward_part(field, axial_bwd, sums, bwd_y, block_len, chunk, i * chunk)
            for i in range(CHUNKS)
        ]
        halos = [exchange(far, near) for _, near, far in sent]
        estimate = [
            part * (own + near + far) / view_count
            for part, (own, _, _), (far, near) in zip(estimate, sent, halos)
        ]
    return jnp.transpose(jnp.concatenate(estimate, axis=0), (1, 0, 2))


def solution(mesh):
    in_specs = (P(None, "slab", "groups", None), P("slab", "groups", None), P(), P(), P())
    out_specs = P("slab", "groups", None)
    return jax.shard_map(body, mesh=mesh, in_specs=in_specs, out_specs=out_specs, check_vma=False)
```

```python
import functools

import jax
import jax.numpy as jnp
from jax import lax
from jax.experimental import pallas as pl
from jax.experimental.pallas import tpu as pltpu
from jax.sharding import PartitionSpec as P

ITERS = 2
CHUNKS = 2
GROUP = 8
VMEM_LIMIT = 16 << 20
ROWS = 16
FORWARD_Z = 2
BACKWARD_Z = 2
QUOTIENT = 2
LANES = 128
F32 = jnp.float32
BF16 = jnp.bfloat16
PRECISE = lax.Precision.HIGHEST


def split(value):
    high = value.astype(BF16)
    low = (value - high.astype(F32)).astype(BF16)
    return high, low


def dot(left, right):
    return jnp.dot(left, right, preferred_element_type=F32)


def normalize(kernel):
    return kernel / jnp.sum(kernel, axis=1, keepdims=True)


def lateral_kernel(taps_x, taps_y, fwd_x, bwd_x, fwd_y, bwd_y, sums_x, sums_y, *, tap_count):
    view_count = taps_x.shape[0]
    size = fwd_x.shape[1]
    rows = lax.broadcasted_iota(jnp.int32, (size, size), 0)
    cols = lax.broadcasted_iota(jnp.int32, (size, size), 1)
    tap_ids = cols - rows + tap_count // 2
    inside = (tap_ids >= 0) & (tap_ids < tap_count)
    for taps, is_x in ((taps_x, True), (taps_y, False)):
        values = taps[...]
        values = values / jnp.sum(values, axis=1, keepdims=True)
        for view in range(view_count):
            line = jnp.broadcast_to(values[view : view + 1, :], (size, size))
            matrix = pltpu.roll(line, size - tap_count // 2, 1, stride=1, stride_axis=0)
            matrix = jnp.where(inside, matrix, 0.0)
            high, low = split(matrix)
            high_t, low_t = split(matrix.T)
            total = jnp.sum(matrix, axis=0, keepdims=True)
            if is_x:
                fwd_x[view] = jnp.concatenate([high, high, low], axis=1)
                bwd_x[view] = jnp.concatenate([high_t, high_t, low_t], axis=1)
                sums_x[view : view + 1, :] = total
            else:
                one = jnp.concatenate([high_t, low_t], axis=1)
                fwd_y[view] = jnp.concatenate([one, one], axis=0)
                one = jnp.concatenate([high, low], axis=1)
                bwd_y[view] = jnp.concatenate([one, one], axis=0)
                sums_y[view : view + 1, :] = total


def lateral_matrices(kernel_x, kernel_y, size_x, size_y):
    view_count, tap_count = kernel_x.shape
    assert size_x == size_y == LANES and tap_count <= size_x
    pads = ((0, 0), (0, size_x - tap_count))
    out = lambda *shape: jax.ShapeDtypeStruct(shape, BF16)
    return pl.pallas_call(
        functools.partial(lateral_kernel, tap_count=tap_count),
        out_shape=(
            out(view_count, size_x, 3 * size_x),
            out(view_count, size_x, 3 * size_x),
            out(view_count, 2 * size_y, 2 * size_y),
            out(view_count, 2 * size_y, 2 * size_y),
            jax.ShapeDtypeStruct((view_count, size_x), F32),
            jax.ShapeDtypeStruct((view_count, size_y), F32),
        ),
        name="lateral_matrices",
    )(jnp.pad(kernel_x, pads), jnp.pad(kernel_y, pads))


def axial_matrices(taps, block_len, odd):
    view_count, tap_count = taps.shape
    reach = tap_count // 2
    base = jnp.arange(block_len)
    near = jnp.where(odd, -block_len, block_len)
    source = jnp.concatenate([base, base + near, base - near])
    tap_ids = source[None, :] - base[:, None] + reach
    pick = (tap_ids[:, :, None] == jnp.arange(tap_count)).astype(F32)
    bands = jnp.einsum("zsk,vk->vzs", pick, taps, precision=PRECISE)
    return bands.reshape(view_count * block_len, -1)


def stacked(matrix):
    high = lax.reduce_precision(matrix, 8, 7)
    low = matrix - high
    return jnp.concatenate([high, high, low], axis=1).astype(BF16)


def totals_kernel(recorded, initial, sums_x, sums_y, weights_z, out, *, block_len):
    view_count = sums_x.shape[0]
    lanes = lax.broadcasted_iota(jnp.int32, out.shape, 1)
    view_of = (lanes % (view_count * block_len)) // block_len
    row_of = lax.broadcasted_iota(jnp.int32, out.shape, 0)
    along_x = sums_x[...]
    weighted = jnp.zeros(sums_y.shape, F32)
    for z in range(block_len):
        part = jnp.dot(along_x, initial[z], precision=PRECISE, preferred_element_type=F32)
        weighted = weighted + part * weights_z[:, z : z + 1]
    weighted = weighted * sums_y[...]
    result = jnp.zeros(out.shape, F32)
    for view in range(view_count):

        def add(z, total):
            return total + jnp.sum(recorded[view * block_len + z].reshape(-1, 8, LANES), axis=0)

        data = lax.fori_loop(0, block_len, add, jnp.zeros((8, LANES), F32), unroll=4)
        blur_total = jnp.sum(weighted[view : view + 1, :])
        data_total = jnp.sum(data)
        value = jnp.where(row_of == 0, data_total, blur_total)
        result = jnp.where(view_of == view, value, result)
    out[...] = result


def totals(recorded, initial, sums_x, sums_y, taps, axis):
    block_len = initial.shape[0]
    view_count, tap_count = taps.shape
    count = lax.axis_size(axis)
    plane = lax.axis_index(axis) * block_len + jnp.arange(block_len)
    target = plane[:, None] + tap_count // 2 - jnp.arange(tap_count)[None, :]
    inside = ((target >= 0) & (target < count * block_len)).astype(F32)
    weights = jnp.sum(taps[:, None, :] * inside[None], axis=2)
    mine = pl.pallas_call(
        functools.partial(totals_kernel, block_len=block_len),
        out_shape=jax.ShapeDtypeStruct((8, 2 * LANES), F32),
        name="totals",
    )(recorded, initial, sums_x, sums_y, weights)
    copies = jnp.broadcast_to(mine[None], (count,) + mine.shape)
    return lax.all_to_all(copies, axis, 0, 0)


def in_vmem(*values):
    return [pltpu.with_memory_space_constraint(value, pltpu.VMEM) for value in values]


def forward_kernel(own, near, far, axial, lateral, out, fields, *, block_len):
    chunk = own.shape[0]
    view_count = lateral.shape[0]
    axial_matrix = axial[...]
    spread = chunk + 1

    def along_z(index, carry):
        start = index * GROUP
        window = jnp.concatenate([ref[pl.ds(start, GROUP)] for ref in (own, near, far)], axis=1)
        high, low = split(window)
        terms = jnp.concatenate([high, low, high], axis=1)
        for pair in range(0, GROUP, 2):
            result = dot(axial_matrix, jnp.concatenate([terms[pair], terms[pair + 1]], axis=1))
            for side in (0, 1):
                row = (start + pair + side) * block_len
                high, low = split(result[:, side * LANES : (side + 1) * LANES])
                for view in range(view_count):
                    part = slice(view * block_len, (view + 1) * block_len)
                    fields[view, pl.ds(row, block_len), :LANES] = high[part]
                    fields[view, pl.ds(row, block_len), LANES:] = low[part]
        return carry

    lax.fori_loop(0, chunk // GROUP, along_z, 0, unroll=FORWARD_Z)

    def along_y(index, carry):
        start = index * ROWS
        for view in range(view_count):
            result = dot(fields[view, pl.ds(start * block_len, ROWS * block_len), :], lateral[view])
            result = result[:, :LANES] + result[:, LANES:]
            for i in range(ROWS):
                first = view * block_len * spread + start + i
                out[pl.ds(first, block_len, stride=spread), :] = result[
                    i * block_len : (i + 1) * block_len
                ]
        return carry

    lax.fori_loop(0, chunk // ROWS, along_y, 0)


def forward_part(own, near, far, axial, lateral):
    chunk, block_len, size_y = own.shape
    view_count = lateral.shape[0]
    return pl.pallas_call(
        functools.partial(forward_kernel, block_len=block_len),
        out_shape=pltpu.VMEM((view_count * block_len * (chunk + 1), size_y), F32),
        scratch_shapes=[pltpu.VMEM((view_count, chunk * block_len, 2 * size_y), BF16)],
        compiler_params=pltpu.CompilerParams(vmem_limit_bytes=VMEM_LIMIT),
        name="forward_part",
    )(*in_vmem(own, near, far, axial, lateral))


def quotient_kernel(*refs, chunks, block_len):
    parts, (recorded, fwd, bwd, out) = refs[:chunks], refs[chunks:]
    view_count = fwd.shape[0]
    planes = view_count * block_len
    size_x = fwd.shape[1]
    chunk = size_x // chunks
    spread = planes + 1

    for view in range(view_count):

        def step(index, carry):
            plane = view * block_len + 2 * index
            field = jnp.concatenate(
                [
                    jnp.concatenate(
                        [ref[pl.ds((plane + side) * (chunk + 1), chunk), :] for ref in parts], axis=0
                    )
                    for side in (0, 1)
                ],
                axis=1,
            )
            high, low = split(field)
            blurred = dot(fwd[view], jnp.concatenate([high, low, high], axis=0))
            data = jnp.concatenate([recorded[plane], recorded[plane + 1]], axis=1)
            high, low = split(data / blurred)
            back = dot(bwd[view], jnp.concatenate([high, low, high], axis=0))
            out[pl.ds(plane, size_x, stride=spread), :] = back[:, :LANES]
            out[pl.ds(plane + 1, size_x, stride=spread), :] = back[:, LANES:]
            return carry

        lax.fori_loop(0, block_len // 2, step, 0, unroll=QUOTIENT)


def quotient_part(parts, recorded, fwd, bwd):
    planes, size_x, size_y = recorded.shape
    view_count = fwd.shape[0]
    return pl.pallas_call(
        functools.partial(quotient_kernel, chunks=len(parts), block_len=planes // view_count),
        out_shape=pltpu.VMEM((size_x * (planes + 1), size_y), F32),
        compiler_params=pltpu.CompilerParams(vmem_limit_bytes=VMEM_LIMIT),
        name="quotient_part",
    )(*in_vmem(*parts, recorded, fwd, bwd))


def backward_kernel(field, axial, sums, lateral, own, near, far, terms, *, block_len, offset):
    chunk = own.shape[0]
    view_count = lateral.shape[0]
    planes = view_count * block_len
    spread = planes + 1
    total = jnp.sum(sums[...], axis=0)
    gains = (total[1:2, :] / total[0:1, :])[:, : axial.shape[1]]
    scaled = axial[...] * gains
    high, low = split(scaled)
    lanes = lax.broadcasted_iota(jnp.int32, scaled.shape, 1)
    axial_matrix = jnp.where(lanes < 2 * planes, high.astype(F32), low.astype(F32)).astype(BF16)

    def along_y(index, carry):
        start = index * ROWS
        for view in range(view_count):
            rows = jnp.concatenate(
                [
                    field[pl.ds((offset + start + i) * spread + view * block_len, block_len), :]
                    for i in range(ROWS)
                ],
                axis=0,
            )
            result = dot(jnp.concatenate(split(rows), axis=1), lateral[view])
            result = result[:, :LANES] + result[:, LANES:]
            high, low = split(result.reshape(ROWS, block_len, LANES))
            for place, part in enumerate((high, low, high)):
                row = place * planes + view * block_len
                terms[pl.ds(start, ROWS), row : row + block_len, :] = part
        return carry

    lax.fori_loop(0, chunk // ROWS, along_y, 0)

    def along_z(index, carry):
        start = index * GROUP
        for pair in range(0, GROUP, 2):
            sent = dot(
                axial_matrix, jnp.concatenate([terms[start + pair], terms[start + pair + 1]], axis=1)
            )
            for side in (0, 1):
                lanes_of = slice(side * LANES, (side + 1) * LANES)
                for place, ref in enumerate((own, near, far)):
                    ref[start + pair + side] = sent[place * block_len : (place + 1) * block_len, lanes_of]
        return carry

    lax.fori_loop(0, chunk // GROUP, along_z, 0, unroll=BACKWARD_Z)


def backward_part(field, axial, sums, lateral, block_len, chunk, offset):
    size_y = field.shape[1]
    planes = lateral.shape[0] * block_len
    shape = pltpu.VMEM((chunk, block_len, size_y), F32)
    return pl.pallas_call(
        functools.partial(backward_kernel, block_len=block_len, offset=offset),
        out_shape=(shape, shape, shape),
        scratch_shapes=[pltpu.VMEM((chunk, 3 * planes, size_y), BF16)],
        compiler_params=pltpu.CompilerParams(vmem_limit_bytes=VMEM_LIMIT),
        name="backward_part",
    )(*in_vmem(field, axial, sums, lateral))


def body(recorded, initial, kernel_x, kernel_y, kernel_z):
    view_count, block_len, size_x, size_y = recorded.shape
    assert kernel_z.shape[1] // 2 <= block_len
    count = lax.axis_size("slab")
    chunk = size_x // CHUNKS
    odd = lax.axis_index("slab") % 2 == 1
    near_pairs = [p for i in range(0, count - 1, 2) for p in ((i, i + 1), (i + 1, i))]
    far_pairs = [p for i in range(1, count - 1, 2) for p in ((i, i + 1), (i + 1, i))]

    def exchange(far_value, near_value):
        return lax.ppermute(far_value, "slab", far_pairs), lax.ppermute(near_value, "slab", near_pairs)

    turned = jnp.transpose(initial, (1, 0, 2))
    estimate = [turned[i * chunk : (i + 1) * chunk] for i in range(CHUNKS)]
    planes = recorded.reshape(view_count * block_len, size_x, size_y)
    fwd_x, bwd_x, fwd_y, bwd_y, sums_x, sums_y = lateral_matrices(kernel_x, kernel_y, size_x, size_y)
    taps_z = normalize(kernel_z)
    bands = axial_matrices(taps_z, block_len, odd)
    axial_fwd = stacked(bands)
    axial_bwd = jnp.concatenate([bands.T] * 3, axis=1)
    sums = totals(planes, initial, sums_x, sums_y, taps_z, "slab")
    for _ in range(ITERS):
        halos = [exchange(part, part) for part in estimate]
        parts = [
            forward_part(part, near, far, axial_fwd, fwd_y)
            for part, (far, near) in zip(estimate, halos)
        ]
        field = quotient_part(parts, planes, fwd_x, bwd_x)
        sent = [
            backward_part(field, axial_bwd, sums, bwd_y, block_len, chunk, i * chunk)
            for i in range(CHUNKS)
        ]
        halos = [exchange(far, near) for _, near, far in sent]
        estimate = [
            part * (own + near + far) / view_count
            for part, (own, _, _), (far, near) in zip(estimate, sent, halos)
        ]
    return jnp.transpose(jnp.concatenate(estimate, axis=0), (1, 0, 2))


def solution(mesh):
    in_specs = (P(None, "slab", "groups", None), P("slab", "groups", None), P(), P(), P())
    out_specs = P("slab", "groups", None)
    return jax.shard_map(body, mesh=mesh, in_specs=in_specs, out_specs=out_specs, check_vma=False)
```

```python
import functools

import jax
import jax.numpy as jnp
from jax import lax
from jax.experimental import pallas as pl
from jax.experimental.pallas import tpu as pltpu
from jax.sharding import PartitionSpec as P


ITERS = 2
GROUP = 8
VMEM_LIMIT = 16 << 20
ROWS = 64
ALONG_Y = 1
FORWARD_Z = 8
BACKWARD_Z = 8
DIVIDE = 8
BACK = 8
LANES = 128
F32 = jnp.float32
BF16 = jnp.bfloat16
PRECISE = lax.Precision.HIGHEST


def split(value):
    high = value.astype(BF16)
    low = (value - high.astype(F32)).astype(BF16)
    return high, low


def dot(left, right):
    return jnp.dot(left, right, preferred_element_type=F32)


def normalized_lines(taps, width):
    view_count, tap_count = taps.shape
    values = jnp.concatenate([taps[...], jnp.zeros((view_count, width - tap_count), F32)], axis=1)
    return values / jnp.sum(values, axis=1, keepdims=True)


def matrices_kernel(
    position, taps_x, taps_y, taps_z, fwd_x, bwd_x, fwd_y, bwd_y, fwd_z, bwd_z, sums_x, sums_y, sums_z, *, count
):
    view_count, tap_count = taps_x.shape
    size = fwd_x.shape[1]
    rows = lax.broadcasted_iota(jnp.int32, (size, size), 0)
    cols = lax.broadcasted_iota(jnp.int32, (size, size), 1)
    tap_ids = cols - rows + tap_count // 2
    inside = (tap_ids >= 0) & (tap_ids < tap_count)
    for taps, is_x in ((taps_x, True), (taps_y, False)):
        values = normalized_lines(taps, size)
        for view in range(view_count):
            line = jnp.broadcast_to(values[view : view + 1, :], (size, size))
            matrix = pltpu.roll(line, size - tap_count // 2, 1, stride=1, stride_axis=0)
            matrix = jnp.where(inside, matrix, 0.0)
            high, low = split(matrix)
            high_t, low_t = split(matrix.T)
            total = jnp.sum(matrix, axis=0, keepdims=True)
            if is_x:
                fwd_x[view] = jnp.concatenate([high, high, low], axis=1)
                bwd_x[view] = jnp.concatenate([high_t, high_t, low_t], axis=1)
                sums_x[view : view + 1, :] = total
            else:
                one = jnp.concatenate([high_t, low_t], axis=1)
                fwd_y[view] = jnp.concatenate([one, one], axis=0)
                one = jnp.concatenate([high, low], axis=1)
                bwd_y[view] = jnp.concatenate([one, one], axis=0)
                sums_y[view : view + 1, :] = total

    block_len = sums_z.shape[1]
    planes = view_count * block_len
    reach = taps_z.shape[1] // 2
    place = position[0]
    odd = (place & 1) == 1
    rows = lax.broadcasted_iota(jnp.int32, (block_len, size), 0)
    cols = lax.broadcasted_iota(jnp.int32, (block_len, size), 1)
    target = place * block_len + rows + reach - cols
    kept = (target >= 0) & (target < count * block_len)
    values = normalized_lines(taps_z, size)
    bands = []
    for view in range(view_count):
        line = jnp.broadcast_to(values[view : view + 1, :], (block_len, size))
        total = jnp.sum(jnp.where(kept, line, 0.0), axis=1, keepdims=True)
        sums_z[view] = jnp.broadcast_to(total, (block_len, size))

        def moved(ahead):
            return pltpu.roll(line, (-ahead) % size, 1, stride=1, stride_axis=0)

        near = jnp.where(odd, moved(reach - 2 * block_len), moved(reach))
        far = jnp.where(odd, moved(reach - block_len), moved(reach - 3 * block_len))
        band = jnp.where(cols < block_len, moved(reach), jnp.where(cols < 2 * block_len, near, far))
        bands.append(jnp.where(cols < 3 * block_len, band, 0.0))
    matrix = jnp.concatenate(bands, axis=0)
    square = jnp.concatenate([matrix, jnp.zeros((size - planes, size), F32)], axis=0)
    blank = jnp.zeros((planes, size), F32)

    def spread(one, two, three):
        wide = [jnp.concatenate([value, blank], axis=1) for value in (one, two, three)]
        return wide[0] + pltpu.roll(wide[1], planes, 1) + pltpu.roll(wide[2], 2 * planes, 1)

    high, low = split(matrix)
    high = high.astype(F32)
    fwd_z[...] = spread(high, high, low.astype(F32)).astype(BF16)
    matrix = square.T[:planes]
    bwd_z[...] = spread(matrix, matrix, matrix)


def matrices(kernel_x, kernel_y, kernel_z, size, block_len, axis):
    view_count, tap_count = kernel_x.shape
    planes = view_count * block_len
    assert size == LANES and tap_count <= size and kernel_y.shape == kernel_x.shape
    assert view_count == 3 and 3 * block_len + kernel_z.shape[1] <= size
    vmem = pl.BlockSpec(memory_space=pltpu.VMEM)
    out = jax.ShapeDtypeStruct
    return pl.pallas_call(
        functools.partial(matrices_kernel, count=lax.axis_size(axis)),
        in_specs=[pl.BlockSpec(memory_space=pltpu.SMEM), vmem, vmem, vmem],
        out_shape=(
            out((view_count, size, 3 * size), BF16),
            out((view_count, size, 3 * size), BF16),
            out((view_count, 2 * size, 2 * size), BF16),
            out((view_count, 2 * size, 2 * size), BF16),
            out((planes, 2 * size), BF16),
            out((planes, 2 * size), F32),
            out((view_count, size), F32),
            out((view_count, size), F32),
            out((view_count, block_len, size), F32),
        ),
        compiler_params=pltpu.CompilerParams(vmem_limit_bytes=VMEM_LIMIT),
        name="matrices",
    )(lax.axis_index(axis).astype(jnp.int32).reshape(1), kernel_x, kernel_y, kernel_z)


def totals_kernel(recorded, initial, sums_x, sums_y, sums_z, out, *, block_len):
    view_count = sums_x.shape[0]
    shape = out.shape
    lanes = lax.broadcasted_iota(jnp.int32, shape, 1)
    view_of = (lanes % (view_count * block_len)) // block_len
    row_of = lax.broadcasted_iota(jnp.int32, shape, 0)
    size_x = initial.shape[1]
    flats = [jnp.zeros((size_x, LANES), F32) for _ in range(view_count)]
    for z in range(block_len):
        plane = initial[z]
        flats = [flat + plane * sums_z[view, z : z + 1, :] for view, flat in enumerate(flats)]
    weighted = jnp.concatenate(
        [
            jnp.dot(sums_x[...], flat, precision=PRECISE, preferred_element_type=F32)[view : view + 1]
            for view, flat in enumerate(flats)
        ],
        axis=0,
    )
    weighted = weighted * sums_y[...]
    result = jnp.zeros(shape, F32)
    for view in range(view_count):

        def add(z, total):
            return total + jnp.sum(recorded[view * block_len + z].reshape(-1, 8, LANES), axis=0)

        data = lax.fori_loop(0, block_len, add, jnp.zeros((8, LANES), F32), unroll=4)
        blur_total = jnp.sum(weighted[view : view + 1, :])
        data_total = jnp.sum(data)
        value = jnp.where(row_of == 0, data_total, blur_total)
        result = jnp.where(view_of == view, value, result)
    out[...] = result


def totals(recorded, initial, sums_x, sums_y, sums_z):
    return pl.pallas_call(
        functools.partial(totals_kernel, block_len=initial.shape[0]),
        out_shape=jax.ShapeDtypeStruct((8, 2 * LANES), F32),
        compiler_params=pltpu.CompilerParams(vmem_limit_bytes=VMEM_LIMIT),
        name="totals",
    )(*in_vmem(recorded), initial, sums_x, sums_y, sums_z)


def summed(value, axis):
    count = lax.axis_size(axis)
    if count & (count - 1):
        return lax.psum(value, axis)
    steps = [1 << bit for bit in range(count.bit_length() - 1)]
    for step in steps[1:2] + steps[:1] + steps[2:]:
        value = value + lax.ppermute(value, axis, [(i, i ^ step) for i in range(count)])
    return value


def in_vmem(*values):
    return [pltpu.with_memory_space_constraint(value, pltpu.VMEM) for value in values]


def forward_kernel(own, near, *refs, block_len):
    *fars, axial, lateral, out, fields = refs
    chunk = own.shape[0]
    view_count = lateral.shape[0]
    axial_matrix = axial[:, : 3 * view_count * block_len]
    spread = chunk + 1

    def along_z(index, carry):
        start = index * GROUP
        far = sum(ref[pl.ds(start, GROUP)] for ref in fars)
        window = jnp.concatenate([own[pl.ds(start, GROUP)], near[pl.ds(start, GROUP)], far], axis=1)
        high, low = split(window)
        terms = jnp.concatenate([high, low, high], axis=1)
        for pair in range(0, GROUP, 2):
            result = dot(axial_matrix, jnp.concatenate([terms[pair], terms[pair + 1]], axis=1))
            for side in (0, 1):
                row = (start + pair + side) * block_len
                high, low = split(result[:, side * LANES : (side + 1) * LANES])
                for view in range(view_count):
                    part = slice(view * block_len, (view + 1) * block_len)
                    fields[view, pl.ds(row, block_len), :LANES] = high[part]
                    fields[view, pl.ds(row, block_len), LANES:] = low[part]
        return carry

    lax.fori_loop(0, chunk // GROUP, along_z, 0, unroll=FORWARD_Z)

    def along_y(index, carry):
        start = index * ROWS
        for view in range(view_count):
            result = dot(fields[view, pl.ds(start * block_len, ROWS * block_len), :], lateral[view])
            result = result[:, :LANES] + result[:, LANES:]
            for i in range(ROWS):
                first = view * block_len * spread + start + i
                out[pl.ds(first, block_len, stride=spread), :] = result[
                    i * block_len : (i + 1) * block_len
                ]
        return carry

    lax.fori_loop(0, chunk // ROWS, along_y, 0, unroll=ALONG_Y)


def forward_part(own, near, fars, axial, lateral):
    chunk, block_len, size_y = own.shape
    view_count = lateral.shape[0]
    return pl.pallas_call(
        functools.partial(forward_kernel, block_len=block_len),
        out_shape=pltpu.VMEM((view_count * block_len * (chunk + 1), size_y), F32),
        scratch_shapes=[pltpu.VMEM((view_count, chunk * block_len, 2 * size_y), BF16)],
        compiler_params=pltpu.CompilerParams(vmem_limit_bytes=VMEM_LIMIT),
        name="forward_part",
    )(*in_vmem(own, near, *fars), axial, *in_vmem(lateral))


def quotient_kernel(*refs, chunks, block_len):
    parts, (recorded, fwd, bwd, out, terms) = refs[:chunks], refs[chunks:]
    view_count = fwd.shape[0]
    planes = view_count * block_len
    size_x = fwd.shape[1]
    chunk = size_x // chunks
    spread = planes + 1

    for view in range(view_count):

        def divide(index, carry):
            plane = view * block_len + 2 * index
            field = jnp.concatenate(
                [
                    jnp.concatenate(
                        [ref[pl.ds((plane + side) * (chunk + 1), chunk), :] for ref in parts], axis=0
                    )
                    for side in (0, 1)
                ],
                axis=1,
            )
            high, low = split(field)
            blurred = dot(fwd[view], jnp.concatenate([high, low, high], axis=0))
            data = jnp.concatenate([recorded[plane], recorded[plane + 1]], axis=1)
            high, low = split(data / blurred)
            terms[index, :size_x] = high
            terms[index, size_x:] = low
            return carry

        lax.fori_loop(0, block_len // 2, divide, 0, unroll=DIVIDE)

        def back(index, carry):
            plane = view * block_len + 2 * index
            both = terms[index]
            result = dot(bwd[view], jnp.concatenate([both, both[:size_x]], axis=0))
            out[pl.ds(plane, size_x, stride=spread), :] = result[:, :LANES]
            out[pl.ds(plane + 1, size_x, stride=spread), :] = result[:, LANES:]
            return carry

        lax.fori_loop(0, block_len // 2, back, 0, unroll=BACK)


def quotient_part(parts, recorded, fwd, bwd):
    planes, size_x, size_y = recorded.shape
    view_count = fwd.shape[0]
    return pl.pallas_call(
        functools.partial(quotient_kernel, chunks=len(parts), block_len=planes // view_count),
        out_shape=pltpu.VMEM((size_x * (planes + 1), size_y), F32),
        scratch_shapes=[pltpu.VMEM((planes // view_count // 2, 2 * size_x, 2 * size_y), BF16)],
        compiler_params=pltpu.CompilerParams(vmem_limit_bytes=VMEM_LIMIT),
        name="quotient_part",
    )(*in_vmem(*parts, recorded, fwd, bwd))


def backward_kernel(field, axial, sums, lateral, own, near, far, terms, *, block_len, offset):
    chunk = own.shape[0]
    view_count = lateral.shape[0]
    planes = view_count * block_len
    spread = planes + 1
    scaled = (axial[...] * (sums[1:2, :] / sums[0:1, :]))[:, : 3 * planes]
    high, low = split(scaled)
    lanes = lax.broadcasted_iota(jnp.int32, scaled.shape, 1)
    axial_matrix = jnp.where(lanes < 2 * planes, high.astype(F32), low.astype(F32)).astype(BF16)

    def along_y(index, carry):
        start = index * ROWS
        for view in range(view_count):
            rows = jnp.concatenate(
                [
                    field[pl.ds((offset + start + i) * spread + view * block_len, block_len), :]
                    for i in range(ROWS)
                ],
                axis=0,
            )
            result = dot(jnp.concatenate(split(rows), axis=1), lateral[view])
            result = result[:, :LANES] + result[:, LANES:]
            high, low = split(result.reshape(ROWS, block_len, LANES))
            for place, part in enumerate((high, low, high)):
                row = place * planes + view * block_len
                terms[pl.ds(start, ROWS), row : row + block_len, :] = part
        return carry

    lax.fori_loop(0, chunk // ROWS, along_y, 0, unroll=ALONG_Y)

    def along_z(index, carry):
        start = index * GROUP
        for pair in range(0, GROUP, 2):
            sent = dot(
                axial_matrix, jnp.concatenate([terms[start + pair], terms[start + pair + 1]], axis=1)
            )
            for side in (0, 1):
                lanes_of = slice(side * LANES, (side + 1) * LANES)
                for place, ref in enumerate((own, near, far)):
                    ref[start + pair + side] = sent[place * block_len : (place + 1) * block_len, lanes_of]
        return carry

    lax.fori_loop(0, chunk // GROUP, along_z, 0, unroll=BACKWARD_Z)


def backward_part(field, axial, sums, lateral, block_len, chunk, offset):
    size_y = field.shape[1]
    planes = lateral.shape[0] * block_len
    shape = pltpu.VMEM((chunk, block_len, size_y), F32)
    return pl.pallas_call(
        functools.partial(backward_kernel, block_len=block_len, offset=offset),
        out_shape=(shape, shape, shape),
        scratch_shapes=[pltpu.VMEM((chunk, 3 * planes, size_y), BF16)],
        compiler_params=pltpu.CompilerParams(vmem_limit_bytes=VMEM_LIMIT),
        name="backward_part",
    )(*in_vmem(field), axial, sums, *in_vmem(lateral))


def body(recorded, initial, kernel_x, kernel_y, kernel_z):
    view_count, block_len, size_x, size_y = recorded.shape
    assert kernel_z.shape[1] // 2 <= block_len
    count = lax.axis_size("slab")
    near_pairs = [p for i in range(0, count - 1, 2) for p in ((i, i + 1), (i + 1, i))]
    first_pairs = [p for i in range(3, count - 1, 4) for p in ((i, i + 1), (i + 1, i))]
    second_pairs = [p for i in range(1, count - 1, 4) for p in ((i, i + 1), (i + 1, i))]

    def swap(value, pairs):
        return lax.ppermute(value, "slab", pairs)

    estimate = jnp.transpose(initial, (1, 0, 2))
    planes = recorded.reshape(view_count * block_len, size_x, size_y)
    fars = [swap(estimate, first_pairs)]
    near = swap(estimate, near_pairs)
    fwd_x, bwd_x, fwd_y, bwd_y, fwd_z, bwd_z, sums_x, sums_y, sums_z = matrices(
        kernel_x, kernel_y, kernel_z, size_x, block_len, "slab"
    )
    sums = totals(planes, initial, sums_x, sums_y, sums_z)
    delayed, sums = lax.optimization_barrier((estimate, sums))
    sums = summed(sums, "slab")
    fars.append(swap(delayed, second_pairs))
    for iteration in range(ITERS):
        if iteration:
            fars = [swap(estimate, first_pairs + second_pairs)]
            near = swap(estimate, near_pairs)
        part = forward_part(estimate, near, fars, fwd_z, fwd_y)
        field = quotient_part([part], planes, fwd_x, bwd_x)
        own, near, far = backward_part(field, bwd_z, sums, bwd_y, block_len, size_x, 0)
        far = swap(far, first_pairs + second_pairs)
        near = swap(near, near_pairs)
        estimate = estimate * (own + near + far) / view_count
    return jnp.transpose(estimate, (1, 0, 2))


def solution(mesh):
    in_specs = (P(None, "slab", "groups", None), P("slab", "groups", None), P(), P(), P())
    out_specs = P("slab", "groups", None)
    return jax.shard_map(body, mesh=mesh, in_specs=in_specs, out_specs=out_specs, check_vma=False)
```

```python
import functools

import jax
import jax.numpy as jnp
from jax import lax
from jax.experimental import pallas as pl
from jax.experimental.pallas import tpu as pltpu
from jax.sharding import PartitionSpec as P


ITERS = 2
GROUP = 8
VMEM_LIMIT = 16 << 20
ROWS = 64
ALONG_Y = 1
FORWARD_Z = 8
BACKWARD_Z = 8
DIVIDE = 8
BACK = 8
LANES = 128
F32 = jnp.float32
BF16 = jnp.bfloat16
PRECISE = lax.Precision.HIGHEST


def split(value):
    high = value.astype(BF16)
    low = (value - high.astype(F32)).astype(BF16)
    return high, low


def dot(left, right):
    return jnp.dot(left, right, preferred_element_type=F32)


def normalized_lines(taps, width):
    view_count, tap_count = taps.shape
    values = jnp.concatenate([taps[...], jnp.zeros((view_count, width - tap_count), F32)], axis=1)
    return values / jnp.sum(values, axis=1, keepdims=True)


def prepare_kernel(
    position, taken_x, taken_y, taken_z, initial_in, recorded_in,
    fwd_x, bwd_x, fwd_y, bwd_y, fwd_z, bwd_z, recorded, out,
    taps_x, taps_y, taps_z, initial, sems, *, count,
):
    view_count, tap_count = taps_x.shape
    block_len = initial.shape[0]
    pairs = [(taken_x, taps_x), (taken_y, taps_y), (taken_z, taps_z), (initial_in, initial)]
    for view in range(view_count):
        part = pl.ds(view * block_len, block_len)
        pairs.append((recorded_in.at[part], recorded.at[part]))
    copies = [pltpu.make_async_copy(*pair, sems.at[i]) for i, pair in enumerate(pairs)]
    for copy in copies:
        copy.start()
    for copy in copies[:3]:
        copy.wait()
    sums_x, sums_y, sums_z = [], [], []
    size = fwd_x.shape[1]
    rows = lax.broadcasted_iota(jnp.int32, (size, size), 0)
    cols = lax.broadcasted_iota(jnp.int32, (size, size), 1)
    tap_ids = cols - rows + tap_count // 2
    inside = (tap_ids >= 0) & (tap_ids < tap_count)
    for taps, is_x in ((taps_x, True), (taps_y, False)):
        values = normalized_lines(taps, size)
        for view in range(view_count):
            line = jnp.broadcast_to(values[view : view + 1, :], (size, size))
            matrix = pltpu.roll(line, size - tap_count // 2, 1, stride=1, stride_axis=0)
            matrix = jnp.where(inside, matrix, 0.0)
            high, low = split(matrix)
            high_t, low_t = split(matrix.T)
            total = jnp.sum(matrix, axis=0, keepdims=True)
            if is_x:
                fwd_x[view] = jnp.concatenate([high, high, low], axis=1)
                bwd_x[view] = jnp.concatenate([high_t, high_t, low_t], axis=1)
                sums_x.append(total)
            else:
                one = jnp.concatenate([high_t, low_t], axis=1)
                fwd_y[view] = jnp.concatenate([one, one], axis=0)
                one = jnp.concatenate([high, low], axis=1)
                bwd_y[view] = jnp.concatenate([one, one], axis=0)
                sums_y.append(total)

    planes = view_count * block_len
    reach = taps_z.shape[1] // 2
    place = position[0]
    odd = (place & 1) == 1
    rows = lax.broadcasted_iota(jnp.int32, (block_len, size), 0)
    cols = lax.broadcasted_iota(jnp.int32, (block_len, size), 1)
    target = place * block_len + rows + reach - cols
    kept = (target >= 0) & (target < count * block_len)
    values = normalized_lines(taps_z, size)
    bands = []
    for view in range(view_count):
        line = jnp.broadcast_to(values[view : view + 1, :], (block_len, size))
        total = jnp.sum(jnp.where(kept, line, 0.0), axis=1, keepdims=True)
        sums_z.append(jnp.broadcast_to(total, (block_len, size)))

        def moved(ahead):
            return pltpu.roll(line, (-ahead) % size, 1, stride=1, stride_axis=0)

        near = jnp.where(odd, moved(reach - 2 * block_len), moved(reach))
        far = jnp.where(odd, moved(reach - block_len), moved(reach - 3 * block_len))
        band = jnp.where(cols < block_len, moved(reach), jnp.where(cols < 2 * block_len, near, far))
        bands.append(jnp.where(cols < 3 * block_len, band, 0.0))
    matrix = jnp.concatenate(bands, axis=0)
    square = jnp.concatenate([matrix, jnp.zeros((size - planes, size), F32)], axis=0)
    blank = jnp.zeros((planes, size), F32)

    def spread(one, two, three):
        wide = [jnp.concatenate([value, blank], axis=1) for value in (one, two, three)]
        return wide[0] + pltpu.roll(wide[1], planes, 1) + pltpu.roll(wide[2], 2 * planes, 1)

    high, low = split(matrix)
    high = high.astype(F32)
    fwd_z[...] = spread(high, high, low.astype(F32)).astype(BF16)
    matrix = square.T[:planes]
    bwd_z[...] = spread(matrix, matrix, matrix)

    copies[3].wait()
    flats = [jnp.zeros((size, LANES), F32) for _ in range(view_count)]
    for z in range(block_len):
        plane = initial[z]
        flats = [flat + plane * sums_z[view][z : z + 1, :] for view, flat in enumerate(flats)]
    lanes = lax.broadcasted_iota(jnp.int32, out.shape, 1)
    view_of = (lanes % planes) // block_len
    row_of = lax.broadcasted_iota(jnp.int32, out.shape, 0)
    result = jnp.zeros(out.shape, F32)
    for view in range(view_count):
        along_x = jnp.broadcast_to(sums_x[view], (8, size))
        weighted = jnp.dot(along_x, flats[view], precision=PRECISE, preferred_element_type=F32)
        blur_total = jnp.sum(weighted[:1] * sums_y[view])
        copies[4 + view].wait()

        def add(z, total):
            return total + jnp.sum(recorded[view * block_len + z].reshape(-1, 8, LANES), axis=0)

        data_total = jnp.sum(lax.fori_loop(0, block_len, add, jnp.zeros((8, LANES), F32), unroll=4))
        value = jnp.where(row_of == 0, data_total, blur_total)
        result = jnp.where(view_of == view, value, result)
    out[...] = result


def prepare(kernel_x, kernel_y, kernel_z, initial, recorded, axis):
    view_count, tap_count = kernel_x.shape
    block_len, size, size_y = initial.shape
    planes = view_count * block_len
    assert size == size_y == LANES and tap_count <= size and kernel_y.shape == kernel_x.shape
    assert view_count == 3 and 3 * block_len + kernel_z.shape[1] <= size
    anywhere = pl.BlockSpec(memory_space=pltpu.HBM)
    out = jax.ShapeDtypeStruct
    return pl.pallas_call(
        functools.partial(prepare_kernel, count=lax.axis_size(axis)),
        in_specs=[pl.BlockSpec(memory_space=pltpu.SMEM)] + [anywhere] * 5,
        out_shape=(
            out((view_count, size, 3 * size), BF16),
            out((view_count, size, 3 * size), BF16),
            pltpu.VMEM((view_count, 2 * size, 2 * size), BF16),
            out((view_count, 2 * size, 2 * size), BF16),
            out((planes, 2 * size), BF16),
            out((planes, 2 * size), F32),
            pltpu.VMEM(recorded.shape, F32),
            out((8, 2 * LANES), F32),
        ),
        scratch_shapes=[
            *(pltpu.VMEM(taps.shape, F32) for taps in (kernel_x, kernel_y, kernel_z)),
            pltpu.VMEM(initial.shape, F32),
            pltpu.SemaphoreType.DMA((4 + view_count,)),
        ],
        compiler_params=pltpu.CompilerParams(vmem_limit_bytes=VMEM_LIMIT),
        name="prepare",
    )(
        lax.axis_index(axis).astype(jnp.int32).reshape(1),
        *(
            pltpu.with_memory_space_constraint(value, pltpu.HBM)
            for value in (kernel_x, kernel_y, kernel_z, initial, recorded)
        ),
    )


def summed(value, axis):
    count = lax.axis_size(axis)
    if count & (count - 1):
        return lax.psum(value, axis)
    steps = [1 << bit for bit in range(count.bit_length() - 1)]
    for step in steps[1:2] + steps[:1] + steps[2:]:
        value = value + lax.ppermute(value, axis, [(i, i ^ step) for i in range(count)])
    return value


def in_vmem(*values):
    return [pltpu.with_memory_space_constraint(value, pltpu.VMEM) for value in values]


def forward_kernel(own, near, *refs, block_len):
    *fars, axial, lateral, out, fields = refs
    chunk = own.shape[0]
    view_count = lateral.shape[0]
    axial_matrix = axial[:, : 3 * view_count * block_len]
    spread = chunk + 1

    def along_z(index, carry):
        start = index * GROUP
        far = sum(ref[pl.ds(start, GROUP)] for ref in fars)
        window = jnp.concatenate([own[pl.ds(start, GROUP)], near[pl.ds(start, GROUP)], far], axis=1)
        high, low = split(window)
        terms = jnp.concatenate([high, low, high], axis=1)
        for pair in range(0, GROUP, 2):
            result = dot(axial_matrix, jnp.concatenate([terms[pair], terms[pair + 1]], axis=1))
            for side in (0, 1):
                row = (start + pair + side) * block_len
                high, low = split(result[:, side * LANES : (side + 1) * LANES])
                for view in range(view_count):
                    part = slice(view * block_len, (view + 1) * block_len)
                    fields[view, pl.ds(row, block_len), :LANES] = high[part]
                    fields[view, pl.ds(row, block_len), LANES:] = low[part]
        return carry

    lax.fori_loop(0, chunk // GROUP, along_z, 0, unroll=FORWARD_Z)

    def along_y(index, carry):
        start = index * ROWS
        for view in range(view_count):
            result = dot(fields[view, pl.ds(start * block_len, ROWS * block_len), :], lateral[view])
            result = result[:, :LANES] + result[:, LANES:]
            for i in range(ROWS):
                first = view * block_len * spread + start + i
                out[pl.ds(first, block_len, stride=spread), :] = result[
                    i * block_len : (i + 1) * block_len
                ]
        return carry

    lax.fori_loop(0, chunk // ROWS, along_y, 0, unroll=ALONG_Y)


def forward_part(own, near, fars, axial, lateral):
    chunk, block_len, size_y = own.shape
    view_count = lateral.shape[0]
    return pl.pallas_call(
        functools.partial(forward_kernel, block_len=block_len),
        out_shape=pltpu.VMEM((view_count * block_len * (chunk + 1), size_y), F32),
        scratch_shapes=[pltpu.VMEM((view_count, chunk * block_len, 2 * size_y), BF16)],
        compiler_params=pltpu.CompilerParams(vmem_limit_bytes=VMEM_LIMIT),
        name="forward_part",
    )(*in_vmem(own, near, *fars), axial, *in_vmem(lateral))


def quotient_kernel(*refs, chunks, block_len):
    parts, (recorded, fwd, bwd, out, terms) = refs[:chunks], refs[chunks:]
    view_count = fwd.shape[0]
    planes = view_count * block_len
    size_x = fwd.shape[1]
    chunk = size_x // chunks
    spread = planes + 1

    for view in range(view_count):

        def divide(index, carry):
            plane = view * block_len + 2 * index
            field = jnp.concatenate(
                [
                    jnp.concatenate(
                        [ref[pl.ds((plane + side) * (chunk + 1), chunk), :] for ref in parts], axis=0
                    )
                    for side in (0, 1)
                ],
                axis=1,
            )
            high, low = split(field)
            blurred = dot(fwd[view], jnp.concatenate([high, low, high], axis=0))
            data = jnp.concatenate([recorded[plane], recorded[plane + 1]], axis=1)
            high, low = split(data / blurred)
            terms[index, :size_x] = high
            terms[index, size_x:] = low
            return carry

        lax.fori_loop(0, block_len // 2, divide, 0, unroll=DIVIDE)

        def back(index, carry):
            plane = view * block_len + 2 * index
            both = terms[index]
            result = dot(bwd[view], jnp.concatenate([both, both[:size_x]], axis=0))
            out[pl.ds(plane, size_x, stride=spread), :] = result[:, :LANES]
            out[pl.ds(plane + 1, size_x, stride=spread), :] = result[:, LANES:]
            return carry

        lax.fori_loop(0, block_len // 2, back, 0, unroll=BACK)


def quotient_part(parts, recorded, fwd, bwd):
    planes, size_x, size_y = recorded.shape
    view_count = fwd.shape[0]
    return pl.pallas_call(
        functools.partial(quotient_kernel, chunks=len(parts), block_len=planes // view_count),
        out_shape=pltpu.VMEM((size_x * (planes + 1), size_y), F32),
        scratch_shapes=[pltpu.VMEM((planes // view_count // 2, 2 * size_x, 2 * size_y), BF16)],
        compiler_params=pltpu.CompilerParams(vmem_limit_bytes=VMEM_LIMIT),
        name="quotient_part",
    )(*in_vmem(*parts, recorded, fwd, bwd))


def backward_kernel(field, axial, sums, lateral, own, near, far, terms, *, block_len, offset):
    chunk = own.shape[0]
    view_count = lateral.shape[0]
    planes = view_count * block_len
    spread = planes + 1
    scaled = (axial[...] * (sums[1:2, :] / sums[0:1, :]))[:, : 3 * planes]
    high, low = split(scaled)
    lanes = lax.broadcasted_iota(jnp.int32, scaled.shape, 1)
    axial_matrix = jnp.where(lanes < 2 * planes, high.astype(F32), low.astype(F32)).astype(BF16)

    def along_y(index, carry):
        start = index * ROWS
        for view in range(view_count):
            rows = jnp.concatenate(
                [
                    field[pl.ds((offset + start + i) * spread + view * block_len, block_len), :]
                    for i in range(ROWS)
                ],
                axis=0,
            )
            result = dot(jnp.concatenate(split(rows), axis=1), lateral[view])
            result = result[:, :LANES] + result[:, LANES:]
            high, low = split(result.reshape(ROWS, block_len, LANES))
            for place, part in enumerate((high, low, high)):
                row = place * planes + view * block_len
                terms[pl.ds(start, ROWS), row : row + block_len, :] = part
        return carry

    lax.fori_loop(0, chunk // ROWS, along_y, 0, unroll=ALONG_Y)

    def along_z(index, carry):
        start = index * GROUP
        for pair in range(0, GROUP, 2):
            sent = dot(
                axial_matrix, jnp.concatenate([terms[start + pair], terms[start + pair + 1]], axis=1)
            )
            for side in (0, 1):
                lanes_of = slice(side * LANES, (side + 1) * LANES)
                for place, ref in enumerate((own, near, far)):
                    ref[start + pair + side] = sent[place * block_len : (place + 1) * block_len, lanes_of]
        return carry

    lax.fori_loop(0, chunk // GROUP, along_z, 0, unroll=BACKWARD_Z)


def backward_part(field, axial, sums, lateral, block_len, chunk, offset):
    size_y = field.shape[1]
    planes = lateral.shape[0] * block_len
    shape = pltpu.VMEM((chunk, block_len, size_y), F32)
    return pl.pallas_call(
        functools.partial(backward_kernel, block_len=block_len, offset=offset),
        out_shape=(shape, shape, shape),
        scratch_shapes=[pltpu.VMEM((chunk, 3 * planes, size_y), BF16)],
        compiler_params=pltpu.CompilerParams(vmem_limit_bytes=VMEM_LIMIT),
        name="backward_part",
    )(*in_vmem(field), axial, sums, *in_vmem(lateral))


def body(recorded, initial, kernel_x, kernel_y, kernel_z):
    view_count, block_len, size_x, size_y = recorded.shape
    assert kernel_z.shape[1] // 2 <= block_len
    count = lax.axis_size("slab")
    near_pairs = [p for i in range(0, count - 1, 2) for p in ((i, i + 1), (i + 1, i))]
    first_pairs = [p for i in range(3, count - 1, 4) for p in ((i, i + 1), (i + 1, i))]
    second_pairs = [p for i in range(1, count - 1, 4) for p in ((i, i + 1), (i + 1, i))]

    def swap(value, pairs):
        return lax.ppermute(value, "slab", pairs)

    estimate = jnp.transpose(initial, (1, 0, 2))
    planes = recorded.reshape(view_count * block_len, size_x, size_y)
    fars = [swap(estimate, first_pairs)]
    near = swap(estimate, near_pairs)
    fwd_x, bwd_x, fwd_y, bwd_y, fwd_z, bwd_z, planes, sums = prepare(
        kernel_x, kernel_y, kernel_z, initial, planes, "slab"
    )
    delayed, sums = lax.optimization_barrier((estimate, sums))
    sums = summed(sums, "slab")
    fars.append(swap(delayed, second_pairs))
    for iteration in range(ITERS):
        if iteration:
            fars = [swap(estimate, first_pairs + second_pairs)]
            near = swap(estimate, near_pairs)
        part = forward_part(estimate, near, fars, fwd_z, fwd_y)
        field = quotient_part([part], planes, fwd_x, bwd_x)
        own, near, far = backward_part(field, bwd_z, sums, bwd_y, block_len, size_x, 0)
        far = swap(far, first_pairs + second_pairs)
        near = swap(near, near_pairs)
        estimate = estimate * (own + near + far) / view_count
    return jnp.transpose(estimate, (1, 0, 2))


def solution(mesh):
    in_specs = (P(None, "slab", "groups", None), P("slab", "groups", None), P(), P(), P())
    out_specs = P("slab", "groups", None)
    return jax.shard_map(body, mesh=mesh, in_specs=in_specs, out_specs=out_specs, check_vma=False)
```

```python
import functools

import jax
import jax.numpy as jnp
from jax import lax
from jax.experimental import pallas as pl
from jax.experimental.pallas import tpu as pltpu
from jax.sharding import PartitionSpec as P


ITERS = 2
GROUP = 8
CHUNKS = 2
VMEM_LIMIT = 16 << 20
ROWS = 64
ALONG_Y = 1
FORWARD_Z = 8
BACKWARD_Z = 8
DIVIDE = 8
BACK = 8
LANES = 128
F32 = jnp.float32
BF16 = jnp.bfloat16
PRECISE = lax.Precision.HIGHEST


def split(value):
    high = value.astype(BF16)
    low = (value - high.astype(F32)).astype(BF16)
    return high, low


def dot(left, right):
    return jnp.dot(left, right, preferred_element_type=F32)


def normalized_lines(taps, width):
    view_count, tap_count = taps.shape
    values = jnp.concatenate([taps[...], jnp.zeros((view_count, width - tap_count), F32)], axis=1)
    return values / jnp.sum(values, axis=1, keepdims=True)


def prepare_kernel(
    position, taken_x, taken_y, taken_z, initial_in, recorded_in,
    fwd_x, bwd_x, fwd_y, bwd_y, fwd_z, bwd_z, recorded, out,
    taps_x, taps_y, taps_z, initial, sems, *, count,
):
    view_count, tap_count = taps_x.shape
    block_len = initial.shape[0]
    pairs = [(taken_x, taps_x), (taken_y, taps_y), (taken_z, taps_z), (initial_in, initial)]
    for view in range(view_count):
        part = pl.ds(view * block_len, block_len)
        pairs.append((recorded_in.at[part], recorded.at[part]))
    copies = [pltpu.make_async_copy(*pair, sems.at[i]) for i, pair in enumerate(pairs)]
    for copy in copies:
        copy.start()
    for copy in copies[:3]:
        copy.wait()
    sums_x, sums_y, sums_z = [], [], []
    size = fwd_x.shape[1]
    rows = lax.broadcasted_iota(jnp.int32, (size, size), 0)
    cols = lax.broadcasted_iota(jnp.int32, (size, size), 1)
    tap_ids = cols - rows + tap_count // 2
    inside = (tap_ids >= 0) & (tap_ids < tap_count)
    for taps, is_x in ((taps_x, True), (taps_y, False)):
        values = normalized_lines(taps, size)
        for view in range(view_count):
            line = jnp.broadcast_to(values[view : view + 1, :], (size, size))
            matrix = pltpu.roll(line, size - tap_count // 2, 1, stride=1, stride_axis=0)
            matrix = jnp.where(inside, matrix, 0.0)
            high, low = split(matrix)
            high_t, low_t = split(matrix.T)
            total = jnp.sum(matrix, axis=0, keepdims=True)
            if is_x:
                fwd_x[view] = jnp.concatenate([high, high, low], axis=1)
                bwd_x[view] = jnp.concatenate([high_t, high_t, low_t], axis=1)
                sums_x.append(total)
            else:
                one = jnp.concatenate([high_t, low_t], axis=1)
                fwd_y[view] = jnp.concatenate([one, one], axis=0)
                one = jnp.concatenate([high, low], axis=1)
                bwd_y[view] = jnp.concatenate([one, one], axis=0)
                sums_y.append(total)

    planes = view_count * block_len
    reach = taps_z.shape[1] // 2
    place = position[0]
    odd = (place & 1) == 1
    rows = lax.broadcasted_iota(jnp.int32, (block_len, size), 0)
    cols = lax.broadcasted_iota(jnp.int32, (block_len, size), 1)
    target = place * block_len + rows + reach - cols
    kept = (target >= 0) & (target < count * block_len)
    values = normalized_lines(taps_z, size)
    bands = []
    for view in range(view_count):
        line = jnp.broadcast_to(values[view : view + 1, :], (block_len, size))
        total = jnp.sum(jnp.where(kept, line, 0.0), axis=1, keepdims=True)
        sums_z.append(jnp.broadcast_to(total, (block_len, size)))

        def moved(ahead):
            return pltpu.roll(line, (-ahead) % size, 1, stride=1, stride_axis=0)

        near = jnp.where(odd, moved(reach - 2 * block_len), moved(reach))
        far = jnp.where(odd, moved(reach - block_len), moved(reach - 3 * block_len))
        band = jnp.where(cols < block_len, moved(reach), jnp.where(cols < 2 * block_len, near, far))
        bands.append(jnp.where(cols < 3 * block_len, band, 0.0))
    matrix = jnp.concatenate(bands, axis=0)
    square = jnp.concatenate([matrix, jnp.zeros((size - planes, size), F32)], axis=0)
    blank = jnp.zeros((planes, size), F32)

    def spread(one, two, three):
        wide = [jnp.concatenate([value, blank], axis=1) for value in (one, two, three)]
        return wide[0] + pltpu.roll(wide[1], planes, 1) + pltpu.roll(wide[2], 2 * planes, 1)

    high, low = split(matrix)
    high = high.astype(F32)
    fwd_z[...] = spread(high, high, low.astype(F32)).astype(BF16)
    matrix = square.T[:planes]
    bwd_z[...] = spread(matrix, matrix, matrix)

    copies[3].wait()
    flats = [jnp.zeros((size, LANES), F32) for _ in range(view_count)]
    for z in range(block_len):
        plane = initial[z]
        flats = [flat + plane * sums_z[view][z : z + 1, :] for view, flat in enumerate(flats)]
    lanes = lax.broadcasted_iota(jnp.int32, out.shape, 1)
    view_of = (lanes % planes) // block_len
    row_of = lax.broadcasted_iota(jnp.int32, out.shape, 0)
    result = jnp.zeros(out.shape, F32)
    for view in range(view_count):
        along_x = jnp.broadcast_to(sums_x[view], (8, size))
        weighted = jnp.dot(along_x, flats[view], precision=PRECISE, preferred_element_type=F32)
        blur_total = jnp.sum(weighted[:1] * sums_y[view])
        copies[4 + view].wait()

        def add(z, total):
            return total + jnp.sum(recorded[view * block_len + z].reshape(-1, 8, LANES), axis=0)

        data_total = jnp.sum(lax.fori_loop(0, block_len, add, jnp.zeros((8, LANES), F32), unroll=4))
        value = jnp.where(row_of == 0, data_total, blur_total)
        result = jnp.where(view_of == view, value, result)
    out[...] = result


def prepare(kernel_x, kernel_y, kernel_z, initial, recorded, axis):
    view_count, tap_count = kernel_x.shape
    block_len, size, size_y = initial.shape
    planes = view_count * block_len
    assert size == size_y == LANES and tap_count <= size and kernel_y.shape == kernel_x.shape
    assert view_count == 3 and 3 * block_len + kernel_z.shape[1] <= size
    anywhere = pl.BlockSpec(memory_space=pltpu.HBM)
    out = jax.ShapeDtypeStruct
    return pl.pallas_call(
        functools.partial(prepare_kernel, count=lax.axis_size(axis)),
        in_specs=[pl.BlockSpec(memory_space=pltpu.SMEM)] + [anywhere] * 5,
        out_shape=(
            out((view_count, size, 3 * size), BF16),
            out((view_count, size, 3 * size), BF16),
            pltpu.VMEM((view_count, 2 * size, 2 * size), BF16),
            out((view_count, 2 * size, 2 * size), BF16),
            out((planes, 2 * size), BF16),
            out((planes, 2 * size), F32),
            pltpu.VMEM(recorded.shape, F32),
            out((8, 2 * LANES), F32),
        ),
        scratch_shapes=[
            *(pltpu.VMEM(taps.shape, F32) for taps in (kernel_x, kernel_y, kernel_z)),
            pltpu.VMEM(initial.shape, F32),
            pltpu.SemaphoreType.DMA((4 + view_count,)),
        ],
        compiler_params=pltpu.CompilerParams(vmem_limit_bytes=VMEM_LIMIT),
        name="prepare",
    )(
        lax.axis_index(axis).astype(jnp.int32).reshape(1),
        *(
            pltpu.with_memory_space_constraint(value, pltpu.HBM)
            for value in (kernel_x, kernel_y, kernel_z, initial, recorded)
        ),
    )


def summed(value, axis):
    count = lax.axis_size(axis)
    if count & (count - 1):
        return lax.psum(value, axis)
    steps = [1 << bit for bit in range(count.bit_length() - 1)]
    for step in steps[1:2] + steps[:1] + steps[2:]:
        value = value + lax.ppermute(value, axis, [(i, i ^ step) for i in range(count)])
    return value


def in_vmem(*values):
    return [pltpu.with_memory_space_constraint(value, pltpu.VMEM) for value in values]


def forward_kernel(*refs, block_len, turned):
    if turned:
        own, near, *fars, axial, lateral, out, fields, planes = refs
        size_x = own.shape[1]
    else:
        *parts, axial, lateral, out, fields = refs
        count = len(parts) // 3
        owns, nears, fars = parts[:count], parts[count : 2 * count], parts[2 * count :]
        chunk = owns[0].shape[0]
        size_x = chunk * count
    view_count = lateral.shape[0]
    axial_matrix = axial[:, : 3 * view_count * block_len]
    spread = size_x + 1
    if turned:
        for place, group in enumerate(([own], [near], fars)):
            for z in range(block_len):
                plane = sum(ref[z] for ref in group)
                planes[pl.ds((place * block_len + z) * spread, size_x), :] = plane

    def window(start, number):
        if turned:
            return jnp.stack([planes[pl.ds(start + i, 3 * block_len, stride=spread), :] for i in range(GROUP)])
        local = pl.ds(start - number * chunk, GROUP)
        return jnp.concatenate([refs_of[number][local] for refs_of in (owns, nears, fars)], axis=1)

    def along_z(index, carry, number):
        start = index * GROUP
        high, low = split(window(start, number))
        terms = jnp.concatenate([high, low, high], axis=1)
        for pair in range(0, GROUP, 2):
            result = dot(axial_matrix, jnp.concatenate([terms[pair], terms[pair + 1]], axis=1))
            for side in (0, 1):
                row = (start + pair + side) * block_len
                high, low = split(result[:, side * LANES : (side + 1) * LANES])
                for view in range(view_count):
                    part = slice(view * block_len, (view + 1) * block_len)
                    fields[view, pl.ds(row, block_len), :LANES] = high[part]
                    fields[view, pl.ds(row, block_len), LANES:] = low[part]
        return carry

    steps = size_x // GROUP // CHUNKS
    for number in range(CHUNKS):
        part_of = functools.partial(along_z, number=number)
        lax.fori_loop(number * steps, (number + 1) * steps, part_of, 0, unroll=FORWARD_Z)

    def along_y(index, carry):
        start = index * ROWS
        for view in range(view_count):
            result = dot(fields[view, pl.ds(start * block_len, ROWS * block_len), :], lateral[view])
            result = result[:, :LANES] + result[:, LANES:]
            for i in range(ROWS):
                first = view * block_len * spread + start + i
                out[pl.ds(first, block_len, stride=spread), :] = result[
                    i * block_len : (i + 1) * block_len
                ]
        return carry

    lax.fori_loop(0, size_x // ROWS, along_y, 0, unroll=ALONG_Y)


def forward_part(parts, axial, lateral, block_len, size_x, turned):
    size_y = parts[0].shape[2]
    view_count = lateral.shape[0]
    scratch = [pltpu.VMEM((view_count, size_x * block_len, 2 * size_y), BF16)]
    if turned:
        scratch.append(pltpu.VMEM((3 * block_len * (size_x + 1), size_y), F32))
    return pl.pallas_call(
        functools.partial(forward_kernel, block_len=block_len, turned=turned),
        out_shape=pltpu.VMEM((view_count * block_len * (size_x + 1), size_y), F32),
        scratch_shapes=scratch,
        compiler_params=pltpu.CompilerParams(vmem_limit_bytes=VMEM_LIMIT),
        name="forward_part",
    )(*in_vmem(*parts), axial, *in_vmem(lateral))


def quotient_kernel(*refs, chunks, block_len):
    parts, (recorded, fwd, bwd, out, terms) = refs[:chunks], refs[chunks:]
    view_count = fwd.shape[0]
    planes = view_count * block_len
    size_x = fwd.shape[1]
    chunk = size_x // chunks
    spread = planes + 1

    for view in range(view_count):

        def divide(index, carry):
            plane = view * block_len + 2 * index
            field = jnp.concatenate(
                [
                    jnp.concatenate(
                        [ref[pl.ds((plane + side) * (chunk + 1), chunk), :] for ref in parts], axis=0
                    )
                    for side in (0, 1)
                ],
                axis=1,
            )
            high, low = split(field)
            blurred = dot(fwd[view], jnp.concatenate([high, low, high], axis=0))
            data = jnp.concatenate([recorded[plane], recorded[plane + 1]], axis=1)
            high, low = split(data / blurred)
            terms[index, :size_x] = high
            terms[index, size_x:] = low
            return carry

        lax.fori_loop(0, block_len // 2, divide, 0, unroll=DIVIDE)

        def back(index, carry):
            plane = view * block_len + 2 * index
            both = terms[index]
            result = dot(bwd[view], jnp.concatenate([both, both[:size_x]], axis=0))
            out[pl.ds(plane, size_x, stride=spread), :] = result[:, :LANES]
            out[pl.ds(plane + 1, size_x, stride=spread), :] = result[:, LANES:]
            return carry

        lax.fori_loop(0, block_len // 2, back, 0, unroll=BACK)


def quotient_part(parts, recorded, fwd, bwd):
    planes, size_x, size_y = recorded.shape
    view_count = fwd.shape[0]
    return pl.pallas_call(
        functools.partial(quotient_kernel, chunks=len(parts), block_len=planes // view_count),
        out_shape=pltpu.VMEM((size_x * (planes + 1), size_y), F32),
        scratch_shapes=[pltpu.VMEM((planes // view_count // 2, 2 * size_x, 2 * size_y), BF16)],
        compiler_params=pltpu.CompilerParams(vmem_limit_bytes=VMEM_LIMIT),
        name="quotient_part",
    )(*in_vmem(*parts, recorded, fwd, bwd))


def backward_kernel(field, axial, sums, lateral, own, near, *refs, block_len):
    *fars, terms = refs
    size_x = own.shape[0]
    chunk = size_x // len(fars)
    view_count = lateral.shape[0]
    planes = view_count * block_len
    spread = planes + 1
    scaled = (axial[...] * (sums[1:2, :] / sums[0:1, :]))[:, : 3 * planes]
    high, low = split(scaled)
    lanes = lax.broadcasted_iota(jnp.int32, scaled.shape, 1)
    axial_matrix = jnp.where(lanes < 2 * planes, high.astype(F32), low.astype(F32)).astype(BF16)

    def along_y(index, carry):
        start = index * ROWS
        for view in range(view_count):
            rows = jnp.concatenate(
                [
                    field[pl.ds((start + i) * spread + view * block_len, block_len), :]
                    for i in range(ROWS)
                ],
                axis=0,
            )
            result = dot(jnp.concatenate(split(rows), axis=1), lateral[view])
            result = result[:, :LANES] + result[:, LANES:]
            high, low = split(result.reshape(ROWS, block_len, LANES))
            for place, part in enumerate((high, low, high)):
                row = place * planes + view * block_len
                terms[pl.ds(start, ROWS), row : row + block_len, :] = part
        return carry

    lax.fori_loop(0, size_x // ROWS, along_y, 0, unroll=ALONG_Y)

    for number, far in enumerate(fars):

        def along_z(index, carry):
            local = index * GROUP
            start = number * chunk + local
            for pair in range(0, GROUP, 2):
                both = jnp.concatenate([terms[start + pair], terms[start + pair + 1]], axis=1)
                sent = dot(axial_matrix, both)
                for side in (0, 1):
                    lanes_of = slice(side * LANES, (side + 1) * LANES)
                    own[start + pair + side] = sent[:block_len, lanes_of]
                    near[start + pair + side] = sent[block_len : 2 * block_len, lanes_of]
                    far[local + pair + side] = sent[2 * block_len :, lanes_of]
            return carry

        lax.fori_loop(0, chunk // GROUP, along_z, 0, unroll=BACKWARD_Z)


def backward_part(field, axial, sums, lateral, block_len, size_x):
    size_y = field.shape[1]
    planes = lateral.shape[0] * block_len
    whole = pltpu.VMEM((size_x, block_len, size_y), F32)
    part = pltpu.VMEM((size_x // CHUNKS, block_len, size_y), F32)
    own, near, *fars = pl.pallas_call(
        functools.partial(backward_kernel, block_len=block_len),
        out_shape=(whole, whole) + (part,) * CHUNKS,
        scratch_shapes=[pltpu.VMEM((size_x, 3 * planes, size_y), BF16)],
        compiler_params=pltpu.CompilerParams(vmem_limit_bytes=VMEM_LIMIT),
        name="backward_part",
    )(*in_vmem(field), axial, sums, *in_vmem(lateral))
    return own, near, fars


def body(recorded, initial, kernel_x, kernel_y, kernel_z):
    view_count, block_len, size_x, size_y = recorded.shape
    assert kernel_z.shape[1] // 2 <= block_len
    count = lax.axis_size("slab")
    near_pairs = [p for i in range(0, count - 1, 2) for p in ((i, i + 1), (i + 1, i))]
    first_pairs = [p for i in range(3, count - 1, 4) for p in ((i, i + 1), (i + 1, i))]
    second_pairs = [p for i in range(1, count - 1, 4) for p in ((i, i + 1), (i + 1, i))]

    def swap(value, pairs):
        return lax.ppermute(value, "slab", pairs)

    planes = recorded.reshape(view_count * block_len, size_x, size_y)
    first = swap(initial, first_pairs)
    near = swap(initial, near_pairs)
    fwd_x, bwd_x, fwd_y, bwd_y, fwd_z, bwd_z, planes, sums = prepare(
        kernel_x, kernel_y, kernel_z, initial, planes, "slab"
    )
    delayed, sums = lax.optimization_barrier((initial, sums))
    sums = summed(sums, "slab")
    parts = [initial, near, first, swap(delayed, second_pairs)]
    chunk = size_x // CHUNKS
    far_pairs = first_pairs + second_pairs
    for iteration in range(ITERS):
        last = iteration == ITERS - 1
        part = forward_part(parts, fwd_z, fwd_y, block_len, size_x, not iteration)
        field = quotient_part([part], planes, fwd_x, bwd_x)
        own, near, fars = backward_part(field, bwd_z, sums, bwd_y, block_len, size_x)
        fars = [swap(far, far_pairs) for far in fars]
        near = swap(near, near_pairs)
        estimate, near_halos, far_halos = [], [], []
        for i, far in enumerate(fars):
            rows = slice(i * chunk, (i + 1) * chunk)
            if i:
                estimate[-1], far = lax.optimization_barrier((estimate[-1], far))
            before = parts[i] if iteration else jnp.transpose(initial[:, rows], (1, 0, 2))
            estimate.append(before * (own[rows] + near[rows] + far) / view_count)
            if not last:
                near_halos.append(swap(estimate[i], near_pairs))
                far_halos.append(swap(estimate[i], far_pairs))
        parts = estimate + near_halos + far_halos
    return jnp.transpose(jnp.concatenate(estimate, axis=0), (1, 0, 2))


def solution(mesh):
    in_specs = (P(None, "slab", "groups", None), P("slab", "groups", None), P(), P(), P())
    out_specs = P("slab", "groups", None)
    return jax.shard_map(body, mesh=mesh, in_specs=in_specs, out_specs=out_specs, check_vma=False)
```

```python
import functools

import jax
import jax.numpy as jnp
from jax import lax
from jax.experimental import pallas as pl
from jax.experimental.pallas import tpu as pltpu
from jax.sharding import PartitionSpec as P


ITERS = 2
GROUP = 8
CHUNKS = 2
VMEM_LIMIT = 16 << 20
ROWS = 64
ALONG_Y = 1
FORWARD_Z = 8
BACKWARD_Z = 8
DIVIDE = 8
BACK = 8
LANES = 128
F32 = jnp.float32
BF16 = jnp.bfloat16
PRECISE = lax.Precision.HIGHEST


def split(value):
    high = value.astype(BF16)
    low = (value - high.astype(F32)).astype(BF16)
    return high, low


def dot(left, right):
    return jnp.dot(left, right, preferred_element_type=F32)


def normalized_lines(taps, width):
    view_count, tap_count = taps.shape
    values = jnp.concatenate([taps[...], jnp.zeros((view_count, width - tap_count), F32)], axis=1)
    return values / jnp.sum(values, axis=1, keepdims=True)


def prepare_kernel(
    position, taken_x, taken_y, taken_z, initial_in, recorded_in,
    fwd_x, bwd_x, fwd_y, bwd_y, fwd_z, bwd_z, recorded, out,
    taps_x, taps_y, taps_z, initial, sems, *, count,
):
    view_count, tap_count = taps_x.shape
    block_len = initial.shape[0]
    pairs = [(taken_x, taps_x), (taken_y, taps_y), (taken_z, taps_z), (initial_in, initial)]
    for view in range(view_count):
        part = pl.ds(view * block_len, block_len)
        pairs.append((recorded_in.at[part], recorded.at[part]))
    copies = [pltpu.make_async_copy(*pair, sems.at[i]) for i, pair in enumerate(pairs)]
    for copy in copies:
        copy.start()
    for copy in copies[:3]:
        copy.wait()
    sums_x, sums_y, sums_z = [], [], []
    size = fwd_x.shape[1]
    rows = lax.broadcasted_iota(jnp.int32, (size, size), 0)
    cols = lax.broadcasted_iota(jnp.int32, (size, size), 1)
    tap_ids = cols - rows + tap_count // 2
    inside = (tap_ids >= 0) & (tap_ids < tap_count)
    for taps, is_x in ((taps_x, True), (taps_y, False)):
        values = normalized_lines(taps, size)
        for view in range(view_count):
            line = jnp.broadcast_to(values[view : view + 1, :], (size, size))
            matrix = pltpu.roll(line, size - tap_count // 2, 1, stride=1, stride_axis=0)
            matrix = jnp.where(inside, matrix, 0.0)
            high, low = split(matrix)
            high_t, low_t = split(matrix.T)
            total = jnp.sum(matrix, axis=0, keepdims=True)
            if is_x:
                fwd_x[view] = jnp.concatenate([high, high, low], axis=1)
                bwd_x[view] = jnp.concatenate([high_t, high_t, low_t], axis=1)
                sums_x.append(total)
            else:
                one = jnp.concatenate([high_t, low_t], axis=1)
                fwd_y[view] = jnp.concatenate([one, one], axis=0)
                one = jnp.concatenate([high, low], axis=1)
                bwd_y[view] = jnp.concatenate([one, one], axis=0)
                sums_y.append(total)

    planes = view_count * block_len
    reach = taps_z.shape[1] // 2
    place = position[0]
    odd = (place & 1) == 1
    rows = lax.broadcasted_iota(jnp.int32, (block_len, size), 0)
    cols = lax.broadcasted_iota(jnp.int32, (block_len, size), 1)
    target = place * block_len + rows + reach - cols
    kept = (target >= 0) & (target < count * block_len)
    values = normalized_lines(taps_z, size)
    bands = []
    for view in range(view_count):
        line = jnp.broadcast_to(values[view : view + 1, :], (block_len, size))
        total = jnp.sum(jnp.where(kept, line, 0.0), axis=1, keepdims=True)
        sums_z.append(jnp.broadcast_to(total, (block_len, size)))

        def moved(ahead):
            return pltpu.roll(line, (-ahead) % size, 1, stride=1, stride_axis=0)

        near = jnp.where(odd, moved(reach - 2 * block_len), moved(reach))
        far = jnp.where(odd, moved(reach - block_len), moved(reach - 3 * block_len))
        band = jnp.where(cols < block_len, moved(reach), jnp.where(cols < 2 * block_len, near, far))
        bands.append(jnp.where(cols < 3 * block_len, band, 0.0))
    matrix = jnp.concatenate(bands, axis=0)
    square = jnp.concatenate([matrix, jnp.zeros((size - planes, size), F32)], axis=0)
    blank = jnp.zeros((planes, size), F32)

    def spread(one, two, three):
        wide = [jnp.concatenate([value, blank], axis=1) for value in (one, two, three)]
        return wide[0] + pltpu.roll(wide[1], planes, 1) + pltpu.roll(wide[2], 2 * planes, 1)

    high, low = split(matrix)
    high = high.astype(F32)
    fwd_z[...] = spread(high, high, low.astype(F32)).astype(BF16)
    matrix = square.T[:planes]
    bwd_z[...] = spread(matrix, matrix, matrix)

    copies[3].wait()
    flats = [jnp.zeros((size, LANES), F32) for _ in range(view_count)]
    for z in range(block_len):
        plane = initial[z]
        flats = [flat + plane * sums_z[view][z : z + 1, :] for view, flat in enumerate(flats)]
    lanes = lax.broadcasted_iota(jnp.int32, out.shape, 1)
    view_of = (lanes % planes) // block_len
    row_of = lax.broadcasted_iota(jnp.int32, out.shape, 0)
    result = jnp.zeros(out.shape, F32)
    for view in range(view_count):
        along_x = jnp.broadcast_to(sums_x[view], (8, size))
        weighted = jnp.dot(along_x, flats[view], precision=PRECISE, preferred_element_type=F32)
        blur_total = jnp.sum(weighted[:1] * sums_y[view])
        copies[4 + view].wait()

        def add(z, total):
            return total + jnp.sum(recorded[view * block_len + z].reshape(-1, 8, LANES), axis=0)

        data_total = jnp.sum(lax.fori_loop(0, block_len, add, jnp.zeros((8, LANES), F32), unroll=4))
        value = jnp.where(row_of == 0, data_total, blur_total)
        result = jnp.where(view_of == view, value, result)
    out[...] = result


def prepare(kernel_x, kernel_y, kernel_z, initial, recorded, axis):
    view_count, tap_count = kernel_x.shape
    block_len, size, size_y = initial.shape
    planes = view_count * block_len
    assert size == size_y == LANES and tap_count <= size and kernel_y.shape == kernel_x.shape
    assert view_count == 3 and 3 * block_len + kernel_z.shape[1] <= size
    anywhere = pl.BlockSpec(memory_space=pltpu.HBM)
    out = jax.ShapeDtypeStruct
    return pl.pallas_call(
        functools.partial(prepare_kernel, count=lax.axis_size(axis)),
        in_specs=[pl.BlockSpec(memory_space=pltpu.SMEM)] + [anywhere] * 5,
        out_shape=(
            out((view_count, size, 3 * size), BF16),
            out((view_count, size, 3 * size), BF16),
            pltpu.VMEM((view_count, 2 * size, 2 * size), BF16),
            out((view_count, 2 * size, 2 * size), BF16),
            out((planes, 2 * size), BF16),
            out((planes, 2 * size), F32),
            pltpu.VMEM(recorded.shape, F32),
            out((8, 2 * LANES), F32),
        ),
        scratch_shapes=[
            *(pltpu.VMEM(taps.shape, F32) for taps in (kernel_x, kernel_y, kernel_z)),
            pltpu.VMEM(initial.shape, F32),
            pltpu.SemaphoreType.DMA((4 + view_count,)),
        ],
        compiler_params=pltpu.CompilerParams(vmem_limit_bytes=VMEM_LIMIT),
        name="prepare",
    )(
        lax.axis_index(axis).astype(jnp.int32).reshape(1),
        *(
            pltpu.with_memory_space_constraint(value, pltpu.HBM)
            for value in (kernel_x, kernel_y, kernel_z, initial, recorded)
        ),
    )


def summed(value, axis):
    count = lax.axis_size(axis)
    if count & (count - 1):
        return lax.psum(value, axis)
    steps = [1 << bit for bit in range(count.bit_length() - 1)]
    for step in steps:
        value = value + lax.ppermute(value, axis, [(i, i ^ step) for i in range(count)])
    return value


def in_vmem(*values):
    return [pltpu.with_memory_space_constraint(value, pltpu.VMEM) for value in values]


def forward_kernel(*refs, block_len, turned):
    if turned:
        own, near, *fars, axial, lateral, out, fields, planes = refs
        size_x = own.shape[1]
    else:
        *parts, axial, lateral, out, fields = refs
        count = len(parts) // 3
        owns, nears, fars = parts[:count], parts[count : 2 * count], parts[2 * count :]
        chunk = owns[0].shape[0]
        size_x = chunk * count
    view_count = lateral.shape[0]
    axial_matrix = axial[:, : 3 * view_count * block_len]
    spread = size_x + 1
    if turned:
        for place, group in enumerate(([own], [near], fars)):
            for z in range(block_len):
                plane = sum(ref[z] for ref in group)
                planes[pl.ds((place * block_len + z) * spread, size_x), :] = plane

    def window(start, number):
        if turned:
            return jnp.stack([planes[pl.ds(start + i, 3 * block_len, stride=spread), :] for i in range(GROUP)])
        local = pl.ds(start - number * chunk, GROUP)
        return jnp.concatenate([refs_of[number][local] for refs_of in (owns, nears, fars)], axis=1)

    def along_z(index, carry, number):
        start = index * GROUP
        high, low = split(window(start, number))
        terms = jnp.concatenate([high, low, high], axis=1)
        for pair in range(0, GROUP, 2):
            result = dot(axial_matrix, jnp.concatenate([terms[pair], terms[pair + 1]], axis=1))
            for side in (0, 1):
                row = (start + pair + side) * block_len
                high, low = split(result[:, side * LANES : (side + 1) * LANES])
                for view in range(view_count):
                    part = slice(view * block_len, (view + 1) * block_len)
                    fields[view, pl.ds(row, block_len), :LANES] = high[part]
                    fields[view, pl.ds(row, block_len), LANES:] = low[part]
        return carry

    steps = size_x // GROUP // CHUNKS
    for number in range(CHUNKS):
        part_of = functools.partial(along_z, number=number)
        lax.fori_loop(number * steps, (number + 1) * steps, part_of, 0, unroll=FORWARD_Z)

    def along_y(index, carry):
        start = index * ROWS
        for view in range(view_count):
            result = dot(fields[view, pl.ds(start * block_len, ROWS * block_len), :], lateral[view])
            result = result[:, :LANES] + result[:, LANES:]
            for i in range(ROWS):
                first = view * block_len * spread + start + i
                out[pl.ds(first, block_len, stride=spread), :] = result[
                    i * block_len : (i + 1) * block_len
                ]
        return carry

    lax.fori_loop(0, size_x // ROWS, along_y, 0, unroll=ALONG_Y)


def forward_part(parts, axial, lateral, block_len, size_x, turned):
    size_y = parts[0].shape[2]
    view_count = lateral.shape[0]
    scratch = [pltpu.VMEM((view_count, size_x * block_len, 2 * size_y), BF16)]
    if turned:
        scratch.append(pltpu.VMEM((3 * block_len * (size_x + 1), size_y), F32))
    return pl.pallas_call(
        functools.partial(forward_kernel, block_len=block_len, turned=turned),
        out_shape=pltpu.VMEM((view_count * block_len * (size_x + 1), size_y), F32),
        scratch_shapes=scratch,
        compiler_params=pltpu.CompilerParams(vmem_limit_bytes=VMEM_LIMIT),
        name="forward_part",
    )(*in_vmem(*parts), axial, *in_vmem(lateral))


def quotient_kernel(*refs, chunks, block_len):
    parts, (recorded, fwd, bwd, out, terms) = refs[:chunks], refs[chunks:]
    view_count = fwd.shape[0]
    planes = view_count * block_len
    size_x = fwd.shape[1]
    chunk = size_x // chunks
    spread = planes + 1

    for view in range(view_count):

        def divide(index, carry):
            plane = view * block_len + 2 * index
            field = jnp.concatenate(
                [
                    jnp.concatenate(
                        [ref[pl.ds((plane + side) * (chunk + 1), chunk), :] for ref in parts], axis=0
                    )
                    for side in (0, 1)
                ],
                axis=1,
            )
            high, low = split(field)
            blurred = dot(fwd[view], jnp.concatenate([high, low, high], axis=0))
            data = jnp.concatenate([recorded[plane], recorded[plane + 1]], axis=1)
            high, low = split(data / blurred)
            terms[index, :size_x] = high
            terms[index, size_x:] = low
            return carry

        lax.fori_loop(0, block_len // 2, divide, 0, unroll=DIVIDE)

        def back(index, carry):
            plane = view * block_len + 2 * index
            both = terms[index]
            result = dot(bwd[view], jnp.concatenate([both, both[:size_x]], axis=0))
            out[pl.ds(plane, size_x, stride=spread), :] = result[:, :LANES]
            out[pl.ds(plane + 1, size_x, stride=spread), :] = result[:, LANES:]
            return carry

        lax.fori_loop(0, block_len // 2, back, 0, unroll=BACK)


def quotient_part(parts, recorded, fwd, bwd):
    planes, size_x, size_y = recorded.shape
    view_count = fwd.shape[0]
    return pl.pallas_call(
        functools.partial(quotient_kernel, chunks=len(parts), block_len=planes // view_count),
        out_shape=pltpu.VMEM((size_x * (planes + 1), size_y), F32),
        scratch_shapes=[pltpu.VMEM((planes // view_count // 2, 2 * size_x, 2 * size_y), BF16)],
        compiler_params=pltpu.CompilerParams(vmem_limit_bytes=VMEM_LIMIT),
        name="quotient_part",
    )(*in_vmem(*parts, recorded, fwd, bwd))


def backward_kernel(field, axial, sums, lateral, own, near, far, terms, *, block_len, offset):
    chunk = own.shape[0]
    view_count = lateral.shape[0]
    planes = view_count * block_len
    spread = planes + 1
    scaled = (axial[...] * (sums[1:2, :] / sums[0:1, :]))[:, : 3 * planes]
    high, low = split(scaled)
    lanes = lax.broadcasted_iota(jnp.int32, scaled.shape, 1)
    axial_matrix = jnp.where(lanes < 2 * planes, high.astype(F32), low.astype(F32)).astype(BF16)

    def along_y(index, carry):
        start = index * ROWS
        for view in range(view_count):
            rows = jnp.concatenate(
                [
                    field[pl.ds((offset + start + i) * spread + view * block_len, block_len), :]
                    for i in range(ROWS)
                ],
                axis=0,
            )
            result = dot(jnp.concatenate(split(rows), axis=1), lateral[view])
            result = result[:, :LANES] + result[:, LANES:]
            high, low = split(result.reshape(ROWS, block_len, LANES))
            for place, part in enumerate((high, low, high)):
                row = place * planes + view * block_len
                terms[pl.ds(start, ROWS), row : row + block_len, :] = part
        return carry

    lax.fori_loop(0, chunk // ROWS, along_y, 0, unroll=ALONG_Y)

    def along_z(index, carry):
        start = index * GROUP
        for pair in range(0, GROUP, 2):
            both = jnp.concatenate([terms[start + pair], terms[start + pair + 1]], axis=1)
            sent = dot(axial_matrix, both)
            for side in (0, 1):
                lanes_of = slice(side * LANES, (side + 1) * LANES)
                for place, ref in enumerate((own, near, far)):
                    ref[start + pair + side] = sent[place * block_len : (place + 1) * block_len, lanes_of]
        return carry

    lax.fori_loop(0, chunk // GROUP, along_z, 0, unroll=BACKWARD_Z)


def backward_part(field, axial, sums, lateral, block_len, chunk, offset):
    size_y = field.shape[1]
    planes = lateral.shape[0] * block_len
    shape = pltpu.VMEM((chunk, block_len, size_y), F32)
    return pl.pallas_call(
        functools.partial(backward_kernel, block_len=block_len, offset=offset),
        out_shape=(shape,) * 3,
        scratch_shapes=[pltpu.VMEM((chunk, 3 * planes, size_y), BF16)],
        compiler_params=pltpu.CompilerParams(vmem_limit_bytes=VMEM_LIMIT),
        name="backward_part",
    )(*in_vmem(field), axial, sums, *in_vmem(lateral))


def finish_kernel(before, own, near, far, *refs, first, view_count):
    out, spread_out, turned, sem = refs[-4:]
    chunk, block_len, _ = before.shape
    spread = chunk + 1
    for i in range(chunk):
        total = own[i] + near[i] + far[i]
        spread_out[pl.ds(i, block_len, stride=spread), :] = before[i] * total / view_count
    for z in range(block_len):
        turned[z] = spread_out[pl.ds(z * spread, chunk), :]
    copy = pltpu.make_async_copy(turned, out.at[:, pl.ds(first, chunk), :], sem)
    copy.start()
    copy.wait()


def finish_part(before, own, near, far, result, first, size_x, view_count):
    chunk, block_len, size_y = before.shape
    vmem = pl.BlockSpec(memory_space=pltpu.VMEM)
    anywhere = pl.BlockSpec(memory_space=pl.ANY)
    extra = [] if result is None else [result]
    return pl.pallas_call(
        functools.partial(finish_kernel, first=first, view_count=view_count),
        in_specs=[vmem] * 4 + [anywhere] * len(extra),
        out_specs=anywhere,
        out_shape=jax.ShapeDtypeStruct((block_len, size_x, size_y), F32),
        scratch_shapes=[
            pltpu.VMEM((block_len * (chunk + 1), size_y), F32),
            pltpu.VMEM((block_len, chunk, size_y), F32),
            pltpu.SemaphoreType.DMA,
        ],
        input_output_aliases={4: 0} if extra else {},
        compiler_params=pltpu.CompilerParams(vmem_limit_bytes=VMEM_LIMIT),
        name="finish_part",
    )(*in_vmem(before, own, near, far), *extra)


def body(recorded, initial, kernel_x, kernel_y, kernel_z):
    view_count, block_len, size_x, size_y = recorded.shape
    assert kernel_z.shape[1] // 2 <= block_len
    count = lax.axis_size("slab")
    near_pairs = [p for i in range(0, count - 1, 2) for p in ((i, i + 1), (i + 1, i))]
    first_pairs = [p for i in range(3, count - 1, 4) for p in ((i, i + 1), (i + 1, i))]
    second_pairs = [p for i in range(1, count - 1, 4) for p in ((i, i + 1), (i + 1, i))]

    def swap(value, pairs):
        return lax.ppermute(value, "slab", pairs)

    planes = recorded.reshape(view_count * block_len, size_x, size_y)
    first = swap(initial, first_pairs)
    near = swap(initial, near_pairs)
    fwd_x, bwd_x, fwd_y, bwd_y, fwd_z, bwd_z, planes, sums = prepare(
        kernel_x, kernel_y, kernel_z, initial, planes, "slab"
    )
    delayed, sums = lax.optimization_barrier((initial, sums))
    sums = summed(sums, "slab")
    parts = [initial, near, first, swap(delayed, second_pairs)]
    chunk = size_x // CHUNKS
    far_pairs = first_pairs + second_pairs
    result = None
    for iteration in range(ITERS):
        last = iteration == ITERS - 1
        part = forward_part(parts, fwd_z, fwd_y, block_len, size_x, not iteration)
        field = quotient_part([part], planes, fwd_x, bwd_x)
        estimate, near_halos, far_halos = [], [], []
        sent = []
        for i in range(CHUNKS):
            sent.append(backward_part(field, bwd_z, sums, bwd_y, block_len, chunk, i * chunk))
        fars = [swap(far, far_pairs) for _, _, far in sent]
        nears = [swap(near, near_pairs) for _, near, _ in sent]
        for i, ((own, _, _), near, far) in enumerate(zip(sent, nears, fars)):
            rows = slice(i * chunk, (i + 1) * chunk)
            if last:
                result = finish_part(parts[i], own, near, far, result, i * chunk, size_x, view_count)
                continue
            if i:
                estimate[-1], far = lax.optimization_barrier((estimate[-1], far))
            before = parts[i] if iteration else jnp.transpose(initial[:, rows], (1, 0, 2))
            estimate.append(before * (own + near + far) / view_count)
            near_halos.append(swap(estimate[i], near_pairs))
            far_halos.append(swap(estimate[i], far_pairs))
        parts = estimate + near_halos + far_halos
    return result


def solution(mesh):
    in_specs = (P(None, "slab", "groups", None), P("slab", "groups", None), P(), P(), P())
    out_specs = P("slab", "groups", None)
    return jax.shard_map(body, mesh=mesh, in_specs=in_specs, out_specs=out_specs, check_vma=False)
```

```python
import functools

import jax
import jax.numpy as jnp
from jax import lax
from jax.experimental import pallas as pl
from jax.experimental.pallas import tpu as pltpu
from jax.sharding import PartitionSpec as P


ITERS = 2
GROUP = 8
CHUNKS = 2
VMEM_LIMIT = 16 << 20
ROWS = 64
ALONG_Y = 1
FORWARD_Z = 8
BACKWARD_Z = 8
DIVIDE = 8
BACK = 8
LANES = 128
F32 = jnp.float32
BF16 = jnp.bfloat16
PRECISE = lax.Precision.HIGHEST


def split(value):
    high = value.astype(BF16)
    low = (value - high.astype(F32)).astype(BF16)
    return high, low


def dot(left, right):
    return jnp.dot(left, right, preferred_element_type=F32)


def normalized_lines(taps, width):
    view_count, tap_count = taps.shape
    values = jnp.concatenate([taps[...], jnp.zeros((view_count, width - tap_count), F32)], axis=1)
    return values / jnp.sum(values, axis=1, keepdims=True)


def prepare_kernel(
    position, taken_x, taken_y, taken_z, initial_in, recorded_in,
    fwd_x, bwd_x, fwd_y, bwd_y, local_z, far_z, bwd_z, recorded, out,
    taps_x, taps_y, taps_z, initial, sems, *, count,
):
    view_count, tap_count = taps_x.shape
    block_len = initial.shape[0]
    pairs = [(taken_x, taps_x), (taken_y, taps_y), (taken_z, taps_z), (initial_in, initial)]
    for view in range(view_count):
        part = pl.ds(view * block_len, block_len)
        pairs.append((recorded_in.at[part], recorded.at[part]))
    copies = [pltpu.make_async_copy(*pair, sems.at[i]) for i, pair in enumerate(pairs)]
    for copy in copies:
        copy.start()
    for copy in copies[:3]:
        copy.wait()
    sums_x, sums_y, sums_z = [], [], []
    size = fwd_x.shape[1]
    rows = lax.broadcasted_iota(jnp.int32, (size, size), 0)
    cols = lax.broadcasted_iota(jnp.int32, (size, size), 1)
    tap_ids = cols - rows + tap_count // 2
    inside = (tap_ids >= 0) & (tap_ids < tap_count)
    for taps, is_x in ((taps_x, True), (taps_y, False)):
        values = normalized_lines(taps, size)
        for view in range(view_count):
            line = jnp.broadcast_to(values[view : view + 1, :], (size, size))
            matrix = pltpu.roll(line, size - tap_count // 2, 1, stride=1, stride_axis=0)
            matrix = jnp.where(inside, matrix, 0.0)
            high, low = split(matrix)
            high_t, low_t = split(matrix.T)
            total = jnp.sum(matrix, axis=0, keepdims=True)
            if is_x:
                fwd_x[view] = jnp.concatenate([high, high, low], axis=1)
                bwd_x[view] = jnp.concatenate([high_t, high_t, low_t], axis=1)
                sums_x.append(total)
            else:
                one = jnp.concatenate([high_t, low_t], axis=1)
                fwd_y[view] = jnp.concatenate([one, one], axis=0)
                one = jnp.concatenate([high, low], axis=1)
                bwd_y[view] = jnp.concatenate([one, one], axis=0)
                sums_y.append(total)

    planes = view_count * block_len
    reach = taps_z.shape[1] // 2
    place = position[0]
    odd = (place & 1) == 1
    rows = lax.broadcasted_iota(jnp.int32, (block_len, size), 0)
    cols = lax.broadcasted_iota(jnp.int32, (block_len, size), 1)
    target = place * block_len + rows + reach - cols
    kept = (target >= 0) & (target < count * block_len)
    values = normalized_lines(taps_z, size)
    bands = []
    for view in range(view_count):
        line = jnp.broadcast_to(values[view : view + 1, :], (block_len, size))
        total = jnp.sum(jnp.where(kept, line, 0.0), axis=1, keepdims=True)
        sums_z.append(jnp.broadcast_to(total, (block_len, size)))

        def moved(ahead):
            return pltpu.roll(line, (-ahead) % size, 1, stride=1, stride_axis=0)

        near = jnp.where(odd, moved(reach - 2 * block_len), moved(reach))
        far = jnp.where(odd, moved(reach - block_len), moved(reach - 3 * block_len))
        band = jnp.where(cols < block_len, moved(reach), jnp.where(cols < 2 * block_len, near, far))
        bands.append(jnp.where(cols < 3 * block_len, band, 0.0))
    matrix = jnp.concatenate(bands, axis=0)
    square = jnp.concatenate([matrix, jnp.zeros((size - planes, size), F32)], axis=0)
    blank = jnp.zeros((planes, size), F32)

    def spread(step, one, two, three):
        wide = [jnp.concatenate([value, blank], axis=1) for value in (one, two, three)]
        return wide[0] + pltpu.roll(wide[1], step, 1) + pltpu.roll(wide[2], 2 * step, 1)

    lanes = lax.broadcasted_iota(jnp.int32, matrix.shape, 1)
    ahead = pltpu.roll(matrix, size - 2 * block_len, 1)
    for ref, value, width in ((local_z, matrix, 2 * block_len), (far_z, ahead, block_len)):
        high, low = split(jnp.where(lanes < width, value, 0.0))
        high = high.astype(F32)
        ref[...] = spread(width, high, high, low.astype(F32)).astype(BF16)
    matrix = square.T[:planes]
    bwd_z[...] = spread(planes, matrix, matrix, matrix)

    copies[3].wait()
    flats = [jnp.zeros((size, LANES), F32) for _ in range(view_count)]
    for z in range(block_len):
        plane = initial[z]
        flats = [flat + plane * sums_z[view][z : z + 1, :] for view, flat in enumerate(flats)]
    lanes = lax.broadcasted_iota(jnp.int32, out.shape, 1)
    view_of = (lanes % planes) // block_len
    row_of = lax.broadcasted_iota(jnp.int32, out.shape, 0)
    result = jnp.zeros(out.shape, F32)
    for view in range(view_count):
        along_x = jnp.broadcast_to(sums_x[view], (8, size))
        weighted = jnp.dot(along_x, flats[view], precision=PRECISE, preferred_element_type=F32)
        blur_total = jnp.sum(weighted[:1] * sums_y[view])
        copies[4 + view].wait()

        def add(z, total):
            return total + jnp.sum(recorded[view * block_len + z].reshape(-1, 8, LANES), axis=0)

        data_total = jnp.sum(lax.fori_loop(0, block_len, add, jnp.zeros((8, LANES), F32), unroll=4))
        value = jnp.where(row_of == 0, data_total, blur_total)
        result = jnp.where(view_of == view, value, result)
    out[...] = result


def prepare(kernel_x, kernel_y, kernel_z, initial, recorded, axis):
    view_count, tap_count = kernel_x.shape
    block_len, size, size_y = initial.shape
    planes = view_count * block_len
    assert size == size_y == LANES and tap_count <= size and kernel_y.shape == kernel_x.shape
    assert view_count == 3 and 3 * block_len + kernel_z.shape[1] <= size
    anywhere = pl.BlockSpec(memory_space=pltpu.HBM)
    out = jax.ShapeDtypeStruct
    return pl.pallas_call(
        functools.partial(prepare_kernel, count=lax.axis_size(axis)),
        in_specs=[pl.BlockSpec(memory_space=pltpu.SMEM)] + [anywhere] * 5,
        out_shape=(
            out((view_count, size, 3 * size), BF16),
            out((view_count, size, 3 * size), BF16),
            pltpu.VMEM((view_count, 2 * size, 2 * size), BF16),
            out((view_count, 2 * size, 2 * size), BF16),
            out((planes, 2 * size), BF16),
            out((planes, 2 * size), BF16),
            out((planes, 2 * size), F32),
            pltpu.VMEM(recorded.shape, F32),
            out((8, 2 * LANES), F32),
        ),
        scratch_shapes=[
            *(pltpu.VMEM(taps.shape, F32) for taps in (kernel_x, kernel_y, kernel_z)),
            pltpu.VMEM(initial.shape, F32),
            pltpu.SemaphoreType.DMA((4 + view_count,)),
        ],
        compiler_params=pltpu.CompilerParams(vmem_limit_bytes=VMEM_LIMIT),
        name="prepare",
    )(
        lax.axis_index(axis).astype(jnp.int32).reshape(1),
        *(
            pltpu.with_memory_space_constraint(value, pltpu.HBM)
            for value in (kernel_x, kernel_y, kernel_z, initial, recorded)
        ),
    )


def summed(value, axis):
    count = lax.axis_size(axis)
    if count & (count - 1):
        return lax.psum(value, axis)
    steps = [1 << bit for bit in range(count.bit_length() - 1)]
    for step in steps:
        value = value + lax.ppermute(value, axis, [(i, i ^ step) for i in range(count)])
    return value


def in_vmem(*values):
    return [pltpu.with_memory_space_constraint(value, pltpu.VMEM) for value in values]


def windows(groups, scratch, turned):
    if not turned:
        chunk = groups[0][0].shape[0]

        def read(start, number):
            local = pl.ds(start - number * chunk, GROUP)
            return jnp.concatenate([group[number][local] for group in groups], axis=1)

        return read
    block_len, size_x, _ = groups[0][0].shape
    spread = size_x + 1
    for place, group in enumerate(groups):
        for z in range(block_len):
            plane = sum(ref[z] for ref in group)
            scratch[pl.ds((place * block_len + z) * spread, size_x), :] = plane
    depth = len(groups) * block_len

    def read_turned(start, number):
        return jnp.stack([scratch[pl.ds(start + i, depth, stride=spread), :] for i in range(GROUP)])

    return read_turned


def by_groups(body, size_x, unroll):
    steps = size_x // GROUP // CHUNKS
    for number in range(CHUNKS):
        lax.fori_loop(
            number * steps, (number + 1) * steps, functools.partial(body, number=number), 0, unroll=unroll
        )


def axial_terms(values):
    high, low = split(values)
    return jnp.concatenate([high, low, high], axis=1)


def local_kernel(*refs, turned):
    *parts, axial, out = refs[:-1] if turned else refs
    half = len(parts) // 2
    read = windows((parts[:half], parts[half:]), refs[-1], turned)
    size_x = out.shape[0]
    depth = parts[0].shape[0 if turned else 1]
    matrix = axial[:, : 6 * depth]

    def along_z(index, carry, number):
        start = index * GROUP
        terms = axial_terms(read(start, number))
        for pair in range(0, GROUP, 2):
            result = dot(matrix, jnp.concatenate([terms[pair], terms[pair + 1]], axis=1))
            out[start + pair] = result[:, :LANES]
            out[start + pair + 1] = result[:, LANES:]
        return carry

    by_groups(along_z, size_x, FORWARD_Z)


def local_part(parts, axial, block_len, size_x, turned):
    size_y = parts[0].shape[2]
    return pl.pallas_call(
        functools.partial(local_kernel, turned=turned),
        out_shape=pltpu.VMEM((size_x, axial.shape[0], size_y), F32),
        scratch_shapes=[pltpu.VMEM((2 * block_len * (size_x + 1), size_y), F32)] * turned,
        compiler_params=pltpu.CompilerParams(vmem_limit_bytes=VMEM_LIMIT),
        name="local_part",
    )(*in_vmem(*parts), axial)


def forward_kernel(*refs, block_len, turned):
    scratch = refs[-1]
    *fars, local, axial, lateral, out, fields = refs[:-1] if turned else refs
    size_x = local.shape[0]
    view_count = lateral.shape[0]
    matrix = axial[:, : 3 * block_len]
    spread = size_x + 1
    read = windows((fars,), scratch, turned)

    def along_z(index, carry, number):
        start = index * GROUP
        terms = axial_terms(read(start, number))
        for pair in range(0, GROUP, 2):
            result = dot(matrix, jnp.concatenate([terms[pair], terms[pair + 1]], axis=1))
            for side in (0, 1):
                row = (start + pair + side) * block_len
                mine = result[:, side * LANES : (side + 1) * LANES] + local[start + pair + side]
                high, low = split(mine)
                for view in range(view_count):
                    part = slice(view * block_len, (view + 1) * block_len)
                    fields[view, pl.ds(row, block_len), :LANES] = high[part]
                    fields[view, pl.ds(row, block_len), LANES:] = low[part]
        return carry

    by_groups(along_z, size_x, FORWARD_Z)

    def along_y(index, carry):
        start = index * ROWS
        for view in range(view_count):
            result = dot(fields[view, pl.ds(start * block_len, ROWS * block_len), :], lateral[view])
            result = result[:, :LANES] + result[:, LANES:]
            for i in range(ROWS):
                first = view * block_len * spread + start + i
                out[pl.ds(first, block_len, stride=spread), :] = result[
                    i * block_len : (i + 1) * block_len
                ]
        return carry

    lax.fori_loop(0, size_x // ROWS, along_y, 0, unroll=ALONG_Y)


def forward_part(fars, local, axial, lateral, block_len, size_x, turned):
    size_y = local.shape[2]
    view_count = lateral.shape[0]
    scratch = [pltpu.VMEM((view_count, size_x * block_len, 2 * size_y), BF16)]
    if turned:
        scratch.append(pltpu.VMEM((block_len * (size_x + 1), size_y), F32))
    return pl.pallas_call(
        functools.partial(forward_kernel, block_len=block_len, turned=turned),
        out_shape=pltpu.VMEM((view_count * block_len * (size_x + 1), size_y), F32),
        scratch_shapes=scratch,
        compiler_params=pltpu.CompilerParams(vmem_limit_bytes=VMEM_LIMIT),
        name="forward_part",
    )(*in_vmem(*fars, local), axial, *in_vmem(lateral))


def quotient_kernel(*refs, chunks, block_len):
    parts, (recorded, fwd, bwd, out, terms) = refs[:chunks], refs[chunks:]
    view_count = fwd.shape[0]
    planes = view_count * block_len
    size_x = fwd.shape[1]
    chunk = size_x // chunks
    spread = planes + 1

    for view in range(view_count):

        def divide(index, carry):
            plane = view * block_len + 2 * index
            field = jnp.concatenate(
                [
                    jnp.concatenate(
                        [ref[pl.ds((plane + side) * (chunk + 1), chunk), :] for ref in parts], axis=0
                    )
                    for side in (0, 1)
                ],
                axis=1,
            )
            high, low = split(field)
            blurred = dot(fwd[view], jnp.concatenate([high, low, high], axis=0))
            data = jnp.concatenate([recorded[plane], recorded[plane + 1]], axis=1)
            high, low = split(data / blurred)
            terms[index, :size_x] = high
            terms[index, size_x:] = low
            return carry

        lax.fori_loop(0, block_len // 2, divide, 0, unroll=DIVIDE)

        def back(index, carry):
            plane = view * block_len + 2 * index
            both = terms[index]
            result = dot(bwd[view], jnp.concatenate([both, both[:size_x]], axis=0))
            out[pl.ds(plane, size_x, stride=spread), :] = result[:, :LANES]
            out[pl.ds(plane + 1, size_x, stride=spread), :] = result[:, LANES:]
            return carry

        lax.fori_loop(0, block_len // 2, back, 0, unroll=BACK)


def quotient_part(parts, recorded, fwd, bwd):
    planes, size_x, size_y = recorded.shape
    view_count = fwd.shape[0]
    return pl.pallas_call(
        functools.partial(quotient_kernel, chunks=len(parts), block_len=planes // view_count),
        out_shape=pltpu.VMEM((size_x * (planes + 1), size_y), F32),
        scratch_shapes=[pltpu.VMEM((planes // view_count // 2, 2 * size_x, 2 * size_y), BF16)],
        compiler_params=pltpu.CompilerParams(vmem_limit_bytes=VMEM_LIMIT),
        name="quotient_part",
    )(*in_vmem(*parts, recorded, fwd, bwd))


def backward_kernel(field, axial, sums, lateral, own, near, far, terms, *, block_len, offset):
    chunk = own.shape[0]
    view_count = lateral.shape[0]
    planes = view_count * block_len
    spread = planes + 1
    scaled = (axial[...] * (sums[1:2, :] / sums[0:1, :]))[:, : 3 * planes]
    high, low = split(scaled)
    lanes = lax.broadcasted_iota(jnp.int32, scaled.shape, 1)
    axial_matrix = jnp.where(lanes < 2 * planes, high.astype(F32), low.astype(F32)).astype(BF16)

    def along_y(index, carry):
        start = index * ROWS
        for view in range(view_count):
            rows = jnp.concatenate(
                [
                    field[pl.ds((offset + start + i) * spread + view * block_len, block_len), :]
                    for i in range(ROWS)
                ],
                axis=0,
            )
            result = dot(jnp.concatenate(split(rows), axis=1), lateral[view])
            result = result[:, :LANES] + result[:, LANES:]
            high, low = split(result.reshape(ROWS, block_len, LANES))
            for place, part in enumerate((high, low, high)):
                row = place * planes + view * block_len
                terms[pl.ds(start, ROWS), row : row + block_len, :] = part
        return carry

    lax.fori_loop(0, chunk // ROWS, along_y, 0, unroll=ALONG_Y)

    def along_z(index, carry):
        start = index * GROUP
        for pair in range(0, GROUP, 2):
            both = jnp.concatenate([terms[start + pair], terms[start + pair + 1]], axis=1)
            sent = dot(axial_matrix, both)
            for side in (0, 1):
                lanes_of = slice(side * LANES, (side + 1) * LANES)
                for place, ref in enumerate((own, near, far)):
                    ref[start + pair + side] = sent[place * block_len : (place + 1) * block_len, lanes_of]
        return carry

    lax.fori_loop(0, chunk // GROUP, along_z, 0, unroll=BACKWARD_Z)


def backward_part(field, axial, sums, lateral, block_len, chunk, offset):
    size_y = field.shape[1]
    planes = lateral.shape[0] * block_len
    shape = pltpu.VMEM((chunk, block_len, size_y), F32)
    return pl.pallas_call(
        functools.partial(backward_kernel, block_len=block_len, offset=offset),
        out_shape=(shape,) * 3,
        scratch_shapes=[pltpu.VMEM((chunk, 3 * planes, size_y), BF16)],
        compiler_params=pltpu.CompilerParams(vmem_limit_bytes=VMEM_LIMIT),
        name="backward_part",
    )(*in_vmem(field), axial, sums, *in_vmem(lateral))


def finish_kernel(before, own, near, far, *refs, first, view_count):
    out, spread_out, turned, sem = refs[-4:]
    chunk, block_len, _ = before.shape
    spread = chunk + 1
    for i in range(chunk):
        total = own[i] + near[i] + far[i]
        spread_out[pl.ds(i, block_len, stride=spread), :] = before[i] * total / view_count
    for z in range(block_len):
        turned[z] = spread_out[pl.ds(z * spread, chunk), :]
    copy = pltpu.make_async_copy(turned, out.at[:, pl.ds(first, chunk), :], sem)
    copy.start()
    copy.wait()


def finish_part(before, own, near, far, result, first, size_x, view_count):
    chunk, block_len, size_y = before.shape
    vmem = pl.BlockSpec(memory_space=pltpu.VMEM)
    anywhere = pl.BlockSpec(memory_space=pl.ANY)
    extra = [] if result is None else [result]
    return pl.pallas_call(
        functools.partial(finish_kernel, first=first, view_count=view_count),
        in_specs=[vmem] * 4 + [anywhere] * len(extra),
        out_specs=anywhere,
        out_shape=jax.ShapeDtypeStruct((block_len, size_x, size_y), F32),
        scratch_shapes=[
            pltpu.VMEM((block_len * (chunk + 1), size_y), F32),
            pltpu.VMEM((block_len, chunk, size_y), F32),
            pltpu.SemaphoreType.DMA,
        ],
        input_output_aliases={4: 0} if extra else {},
        compiler_params=pltpu.CompilerParams(vmem_limit_bytes=VMEM_LIMIT),
        name="finish_part",
    )(*in_vmem(before, own, near, far), *extra)


def body(recorded, initial, kernel_x, kernel_y, kernel_z):
    view_count, block_len, size_x, size_y = recorded.shape
    assert kernel_z.shape[1] // 2 <= block_len
    count = lax.axis_size("slab")
    near_pairs = [p for i in range(0, count - 1, 2) for p in ((i, i + 1), (i + 1, i))]
    first_pairs = [p for i in range(3, count - 1, 4) for p in ((i, i + 1), (i + 1, i))]
    second_pairs = [p for i in range(1, count - 1, 4) for p in ((i, i + 1), (i + 1, i))]

    def swap(value, pairs):
        return lax.ppermute(value, "slab", pairs)

    planes = recorded.reshape(view_count * block_len, size_x, size_y)
    first = swap(initial, first_pairs)
    near = swap(initial, near_pairs)
    fwd_x, bwd_x, fwd_y, bwd_y, local_z, far_z, bwd_z, planes, sums = prepare(
        kernel_x, kernel_y, kernel_z, initial, planes, "slab"
    )
    delayed, sums = lax.optimization_barrier((initial, sums))
    sums = summed(sums, "slab")
    inner = [initial, near]
    far_halos = [first, swap(delayed, second_pairs)]
    chunk = size_x // CHUNKS
    far_pairs = first_pairs + second_pairs
    result = None
    for iteration in range(ITERS):
        last = iteration == ITERS - 1
        local = local_part(inner, local_z, block_len, size_x, not iteration)
        part = forward_part(far_halos, local, far_z, fwd_y, block_len, size_x, not iteration)
        field = quotient_part([part], planes, fwd_x, bwd_x)
        estimate, near_halos, far_halos = [], [], []
        sent = []
        for i in range(CHUNKS):
            sent.append(backward_part(field, bwd_z, sums, bwd_y, block_len, chunk, i * chunk))
        fars = [swap(far, far_pairs) for _, _, far in sent]
        nears = [swap(near, near_pairs) for _, near, _ in sent]
        for i, ((own, _, _), near, far) in enumerate(zip(sent, nears, fars)):
            rows = slice(i * chunk, (i + 1) * chunk)
            if last:
                result = finish_part(inner[i], own, near, far, result, i * chunk, size_x, view_count)
                continue
            if i:
                estimate[-1], far = lax.optimization_barrier((estimate[-1], far))
            before = inner[i] if iteration else jnp.transpose(initial[:, rows], (1, 0, 2))
            estimate.append(before * (own + near + far) / view_count)
            near_halos.append(swap(estimate[i], near_pairs))
            far_halos.append(swap(estimate[i], far_pairs))
        inner = estimate + near_halos
    return result


def solution(mesh):
    in_specs = (P(None, "slab", "groups", None), P("slab", "groups", None), P(), P(), P())
    out_specs = P("slab", "groups", None)
    return jax.shard_map(body, mesh=mesh, in_specs=in_specs, out_specs=out_specs, check_vma=False)
```

```python
import functools

import jax
import jax.numpy as jnp
from jax import lax
from jax.experimental import pallas as pl
from jax.experimental.pallas import tpu as pltpu
from jax.sharding import PartitionSpec as P


ITERS = 2
GROUP = 8
SENT = 4
CHUNKS = 2
VMEM_LIMIT = 16 << 20
ROWS = 64
ALONG_Y = 1
FORWARD_Z = 8
BACKWARD_Z = 8
DIVIDE = 8
BACK = 8
LANES = 128
F32 = jnp.float32
BF16 = jnp.bfloat16
PRECISE = lax.Precision.HIGHEST


def split(value):
    high = value.astype(BF16)
    low = (value - high.astype(F32)).astype(BF16)
    return high, low


def dot(left, right):
    return jnp.dot(left, right, preferred_element_type=F32)


def normalized_lines(taps, width):
    view_count, tap_count = taps.shape
    values = jnp.concatenate([taps[...], jnp.zeros((view_count, width - tap_count), F32)], axis=1)
    return values / jnp.sum(values, axis=1, keepdims=True)


def prepare_kernel(
    position, taken_x, taken_y, taken_z, initial_in, recorded_in,
    fwd_x, bwd_x, fwd_y, bwd_y, local_z, far_z, bwd_z, recorded, out,
    taps_x, taps_y, taps_z, initial, sems, *, count,
):
    view_count, tap_count = taps_x.shape
    block_len = initial.shape[0]
    pairs = [(taken_x, taps_x), (taken_y, taps_y), (taken_z, taps_z), (initial_in, initial)]
    for view in range(view_count):
        part = pl.ds(view * block_len, block_len)
        pairs.append((recorded_in.at[part], recorded.at[part]))
    copies = [pltpu.make_async_copy(*pair, sems.at[i]) for i, pair in enumerate(pairs)]
    for copy in copies:
        copy.start()
    for copy in copies[:3]:
        copy.wait()
    sums_x, sums_y, sums_z = [], [], []
    size = fwd_x.shape[1]
    rows = lax.broadcasted_iota(jnp.int32, (size, size), 0)
    cols = lax.broadcasted_iota(jnp.int32, (size, size), 1)
    tap_ids = cols - rows + tap_count // 2
    inside = (tap_ids >= 0) & (tap_ids < tap_count)
    for taps, is_x in ((taps_x, True), (taps_y, False)):
        values = normalized_lines(taps, size)
        for view in range(view_count):
            line = jnp.broadcast_to(values[view : view + 1, :], (size, size))
            matrix = pltpu.roll(line, size - tap_count // 2, 1, stride=1, stride_axis=0)
            matrix = jnp.where(inside, matrix, 0.0)
            high, low = split(matrix)
            high_t, low_t = split(matrix.T)
            total = jnp.sum(matrix, axis=0, keepdims=True)
            if is_x:
                fwd_x[view] = jnp.concatenate([high, high, low], axis=1)
                bwd_x[view] = jnp.concatenate([high_t, high_t, low_t], axis=1)
                sums_x.append(total)
            else:
                one = jnp.concatenate([high_t, low_t], axis=1)
                fwd_y[view] = jnp.concatenate([one, one], axis=0)
                one = jnp.concatenate([high, low], axis=1)
                bwd_y[view] = jnp.concatenate([one, one], axis=0)
                sums_y.append(total)

    planes = view_count * block_len
    reach = taps_z.shape[1] // 2
    place = position[0]
    odd = (place & 1) == 1
    rows = lax.broadcasted_iota(jnp.int32, (block_len, size), 0)
    cols = lax.broadcasted_iota(jnp.int32, (block_len, size), 1)
    target = place * block_len + rows + reach - cols
    kept = (target >= 0) & (target < count * block_len)
    values = normalized_lines(taps_z, size)
    bands = []
    for view in range(view_count):
        line = jnp.broadcast_to(values[view : view + 1, :], (block_len, size))
        total = jnp.sum(jnp.where(kept, line, 0.0), axis=1, keepdims=True)
        sums_z.append(jnp.broadcast_to(total, (block_len, size)))

        def moved(ahead):
            return pltpu.roll(line, (-ahead) % size, 1, stride=1, stride_axis=0)

        near = jnp.where(odd, moved(reach - 2 * block_len), moved(reach))
        far = jnp.where(odd, moved(reach - block_len), moved(reach - 3 * block_len))
        band = jnp.where(cols < block_len, moved(reach), jnp.where(cols < 2 * block_len, near, far))
        bands.append(jnp.where(cols < 3 * block_len, band, 0.0))
    matrix = jnp.concatenate(bands, axis=0)
    square = jnp.concatenate([matrix, jnp.zeros((size - planes, size), F32)], axis=0)
    blank = jnp.zeros((planes, size), F32)

    def spread(step, one, two, three):
        wide = [jnp.concatenate([value, blank], axis=1) for value in (one, two, three)]
        return wide[0] + pltpu.roll(wide[1], step, 1) + pltpu.roll(wide[2], 2 * step, 1)

    lanes = lax.broadcasted_iota(jnp.int32, matrix.shape, 1)
    ahead = pltpu.roll(matrix, size - 2 * block_len, 1)
    for ref, value, width in ((local_z, matrix, 2 * block_len), (far_z, ahead, block_len)):
        high, low = split(jnp.where(lanes < width, value, 0.0))
        high = high.astype(F32)
        ref[...] = spread(width, high, high, low.astype(F32)).astype(BF16)
    matrix = square.T[:planes]
    bwd_z[...] = spread(planes, matrix, matrix, matrix)

    copies[3].wait()
    flats = [jnp.zeros((size, LANES), F32) for _ in range(view_count)]
    for z in range(block_len):
        plane = initial[z]
        flats = [flat + plane * sums_z[view][z : z + 1, :] for view, flat in enumerate(flats)]
    lanes = lax.broadcasted_iota(jnp.int32, out.shape, 1)
    view_of = (lanes % planes) // block_len
    row_of = lax.broadcasted_iota(jnp.int32, out.shape, 0)
    result = jnp.zeros(out.shape, F32)
    for view in range(view_count):
        along_x = jnp.broadcast_to(sums_x[view], (8, size))
        weighted = jnp.dot(along_x, flats[view], precision=PRECISE, preferred_element_type=F32)
        blur_total = jnp.sum(weighted[:1] * sums_y[view])
        copies[4 + view].wait()

        def add(z, total):
            return total + jnp.sum(recorded[view * block_len + z].reshape(-1, 8, LANES), axis=0)

        data_total = jnp.sum(lax.fori_loop(0, block_len, add, jnp.zeros((8, LANES), F32), unroll=4))
        value = jnp.where(row_of == 0, data_total, blur_total)
        result = jnp.where(view_of == view, value, result)
    out[...] = result


def prepare(kernel_x, kernel_y, kernel_z, initial, recorded, axis):
    view_count, tap_count = kernel_x.shape
    block_len, size, size_y = initial.shape
    planes = view_count * block_len
    assert size == size_y == LANES and tap_count <= size and kernel_y.shape == kernel_x.shape
    assert view_count == 3 and 3 * block_len + kernel_z.shape[1] <= size
    anywhere = pl.BlockSpec(memory_space=pltpu.HBM)
    out = jax.ShapeDtypeStruct
    return pl.pallas_call(
        functools.partial(prepare_kernel, count=lax.axis_size(axis)),
        in_specs=[pl.BlockSpec(memory_space=pltpu.SMEM)] + [anywhere] * 5,
        out_shape=(
            out((view_count, size, 3 * size), BF16),
            out((view_count, size, 3 * size), BF16),
            pltpu.VMEM((view_count, 2 * size, 2 * size), BF16),
            out((view_count, 2 * size, 2 * size), BF16),
            out((planes, 2 * size), BF16),
            out((planes, 2 * size), BF16),
            out((planes, 2 * size), F32),
            pltpu.VMEM(recorded.shape, F32),
            out((8, 2 * LANES), F32),
        ),
        scratch_shapes=[
            *(pltpu.VMEM(taps.shape, F32) for taps in (kernel_x, kernel_y, kernel_z)),
            pltpu.VMEM(initial.shape, F32),
            pltpu.SemaphoreType.DMA((4 + view_count,)),
        ],
        compiler_params=pltpu.CompilerParams(vmem_limit_bytes=VMEM_LIMIT),
        name="prepare",
    )(
        lax.axis_index(axis).astype(jnp.int32).reshape(1),
        *(
            pltpu.with_memory_space_constraint(value, pltpu.HBM)
            for value in (kernel_x, kernel_y, kernel_z, initial, recorded)
        ),
    )


def summed(value, axis):
    count = lax.axis_size(axis)
    if count & (count - 1):
        return lax.psum(value, axis)
    steps = [1 << bit for bit in range(count.bit_length() - 1)]
    for step in steps:
        value = value + lax.ppermute(value, axis, [(i, i ^ step) for i in range(count)])
    return value


def in_vmem(*values):
    return [pltpu.with_memory_space_constraint(value, pltpu.VMEM) for value in values]


def windows(groups, scratch, turned):
    if not turned:
        chunk = groups[0][0].shape[0]

        def read(start, number):
            local = pl.ds(start - number * chunk, GROUP)
            return jnp.concatenate([group[number][local] for group in groups], axis=1)

        return read
    block_len, size_x, _ = groups[0][0].shape
    spread = size_x + 1
    for place, group in enumerate(groups):
        for z in range(block_len):
            plane = sum(ref[z] for ref in group)
            scratch[pl.ds((place * block_len + z) * spread, size_x), :] = plane
    depth = len(groups) * block_len

    def read_turned(start, number):
        return jnp.stack([scratch[pl.ds(start + i, depth, stride=spread), :] for i in range(GROUP)])

    return read_turned


def by_groups(body, size_x, unroll):
    steps = size_x // GROUP // CHUNKS
    for number in range(CHUNKS):
        lax.fori_loop(
            number * steps, (number + 1) * steps, functools.partial(body, number=number), 0, unroll=unroll
        )


def axial_terms(values):
    high, low = split(values)
    return jnp.concatenate([high, low, high], axis=1)


def local_kernel(*refs, turned):
    *parts, axial, out = refs[:-1] if turned else refs
    half = len(parts) // 2
    read = windows((parts[:half], parts[half:]), refs[-1], turned)
    size_x = out.shape[0]
    depth = parts[0].shape[0 if turned else 1]
    matrix = axial[:, : 6 * depth]

    def along_z(index, carry, number):
        start = index * GROUP
        terms = axial_terms(read(start, number))
        for pair in range(0, GROUP, 2):
            result = dot(matrix, jnp.concatenate([terms[pair], terms[pair + 1]], axis=1))
            out[start + pair] = result[:, :LANES]
            out[start + pair + 1] = result[:, LANES:]
        return carry

    by_groups(along_z, size_x, FORWARD_Z)


def local_part(parts, axial, block_len, size_x, turned):
    size_y = parts[0].shape[2]
    return pl.pallas_call(
        functools.partial(local_kernel, turned=turned),
        out_shape=pltpu.VMEM((size_x, axial.shape[0], size_y), F32),
        scratch_shapes=[pltpu.VMEM((2 * block_len * (size_x + 1), size_y), F32)] * turned,
        compiler_params=pltpu.CompilerParams(vmem_limit_bytes=VMEM_LIMIT),
        name="local_part",
    )(*in_vmem(*parts), axial)


def forward_kernel(*refs, block_len, turned):
    scratch = refs[-1]
    *fars, local, axial, lateral, out, fields = refs[:-1] if turned else refs
    size_x = local.shape[0]
    view_count = lateral.shape[0]
    matrix = axial[:, : 3 * block_len]
    spread = size_x + 1
    read = windows((fars,), scratch, turned)

    def along_z(index, carry, number):
        start = index * GROUP
        terms = axial_terms(read(start, number))
        for pair in range(0, GROUP, 2):
            result = dot(matrix, jnp.concatenate([terms[pair], terms[pair + 1]], axis=1))
            for side in (0, 1):
                row = (start + pair + side) * block_len
                mine = result[:, side * LANES : (side + 1) * LANES] + local[start + pair + side]
                high, low = split(mine)
                for view in range(view_count):
                    part = slice(view * block_len, (view + 1) * block_len)
                    fields[view, pl.ds(row, block_len), :LANES] = high[part]
                    fields[view, pl.ds(row, block_len), LANES:] = low[part]
        return carry

    by_groups(along_z, size_x, FORWARD_Z)

    def along_y(index, carry):
        start = index * ROWS
        for view in range(view_count):
            result = dot(fields[view, pl.ds(start * block_len, ROWS * block_len), :], lateral[view])
            result = result[:, :LANES] + result[:, LANES:]
            for i in range(ROWS):
                first = view * block_len * spread + start + i
                out[pl.ds(first, block_len, stride=spread), :] = result[
                    i * block_len : (i + 1) * block_len
                ]
        return carry

    lax.fori_loop(0, size_x // ROWS, along_y, 0, unroll=ALONG_Y)


def forward_part(fars, local, axial, lateral, block_len, size_x, turned):
    size_y = local.shape[2]
    view_count = lateral.shape[0]
    scratch = [pltpu.VMEM((view_count, size_x * block_len, 2 * size_y), BF16)]
    if turned:
        scratch.append(pltpu.VMEM((block_len * (size_x + 1), size_y), F32))
    return pl.pallas_call(
        functools.partial(forward_kernel, block_len=block_len, turned=turned),
        out_shape=pltpu.VMEM((view_count * block_len * (size_x + 1), size_y), F32),
        scratch_shapes=scratch,
        compiler_params=pltpu.CompilerParams(vmem_limit_bytes=VMEM_LIMIT),
        name="forward_part",
    )(*in_vmem(*fars, local), axial, *in_vmem(lateral))


def quotient_kernel(*refs, chunks, block_len):
    parts, (recorded, fwd, bwd, out, terms) = refs[:chunks], refs[chunks:]
    view_count = fwd.shape[0]
    planes = view_count * block_len
    size_x = fwd.shape[1]
    chunk = size_x // chunks
    spread = planes + 1

    for view in range(view_count):

        def divide(index, carry):
            plane = view * block_len + 2 * index
            field = jnp.concatenate(
                [
                    jnp.concatenate(
                        [ref[pl.ds((plane + side) * (chunk + 1), chunk), :] for ref in parts], axis=0
                    )
                    for side in (0, 1)
                ],
                axis=1,
            )
            high, low = split(field)
            blurred = dot(fwd[view], jnp.concatenate([high, low, high], axis=0))
            data = jnp.concatenate([recorded[plane], recorded[plane + 1]], axis=1)
            high, low = split(data / blurred)
            terms[index, :size_x] = high
            terms[index, size_x:] = low
            return carry

        lax.fori_loop(0, block_len // 2, divide, 0, unroll=DIVIDE)

        def back(index, carry):
            plane = view * block_len + 2 * index
            both = terms[index]
            result = dot(bwd[view], jnp.concatenate([both, both[:size_x]], axis=0))
            out[pl.ds(plane, size_x, stride=spread), :] = result[:, :LANES]
            out[pl.ds(plane + 1, size_x, stride=spread), :] = result[:, LANES:]
            return carry

        lax.fori_loop(0, block_len // 2, back, 0, unroll=BACK)


def quotient_part(parts, recorded, fwd, bwd):
    planes, size_x, size_y = recorded.shape
    view_count = fwd.shape[0]
    return pl.pallas_call(
        functools.partial(quotient_kernel, chunks=len(parts), block_len=planes // view_count),
        out_shape=pltpu.VMEM((size_x * (planes + 1), size_y), F32),
        scratch_shapes=[pltpu.VMEM((planes // view_count // 2, 2 * size_x, 2 * size_y), BF16)],
        compiler_params=pltpu.CompilerParams(vmem_limit_bytes=VMEM_LIMIT),
        name="quotient_part",
    )(*in_vmem(*parts, recorded, fwd, bwd))


def backward_kernel(field, axial, sums, lateral, own, near, far, terms, *, block_len, offset):
    chunk = own.shape[0]
    view_count = lateral.shape[0]
    planes = view_count * block_len
    spread = planes + 1
    scaled = (axial[...] * (sums[1:2, :] / sums[0:1, :]))[:, : 3 * planes]
    high, low = split(scaled)
    lanes = lax.broadcasted_iota(jnp.int32, scaled.shape, 1)
    axial_matrix = jnp.where(lanes < 2 * planes, high.astype(F32), low.astype(F32)).astype(BF16)

    def along_y(index, carry):
        start = index * ROWS
        for view in range(view_count):
            rows = jnp.concatenate(
                [
                    field[pl.ds((offset + start + i) * spread + view * block_len, block_len), :]
                    for i in range(ROWS)
                ],
                axis=0,
            )
            result = dot(jnp.concatenate(split(rows), axis=1), lateral[view])
            result = result[:, :LANES] + result[:, LANES:]
            high, low = split(result.reshape(ROWS, block_len, LANES))
            for place, part in enumerate((high, low, high)):
                row = place * planes + view * block_len
                terms[pl.ds(start, ROWS), row : row + block_len, :] = part
        return carry

    lax.fori_loop(0, chunk // ROWS, along_y, 0, unroll=ALONG_Y)

    def along_z(index, carry):
        start = index * GROUP
        for pair in range(0, GROUP, 2):
            both = jnp.concatenate([terms[start + pair], terms[start + pair + 1]], axis=1)
            sent = dot(axial_matrix, both)
            for side in (0, 1):
                lanes_of = slice(side * LANES, (side + 1) * LANES)
                for place, ref in enumerate((own, near, far)):
                    ref[start + pair + side] = sent[place * block_len : (place + 1) * block_len, lanes_of]
        return carry

    lax.fori_loop(0, chunk // GROUP, along_z, 0, unroll=BACKWARD_Z)


def backward_part(field, axial, sums, lateral, block_len, chunk, offset):
    size_y = field.shape[1]
    planes = lateral.shape[0] * block_len
    shape = pltpu.VMEM((chunk, block_len, size_y), F32)
    return pl.pallas_call(
        functools.partial(backward_kernel, block_len=block_len, offset=offset),
        out_shape=(shape,) * 3,
        scratch_shapes=[pltpu.VMEM((chunk, 3 * planes, size_y), BF16)],
        compiler_params=pltpu.CompilerParams(vmem_limit_bytes=VMEM_LIMIT),
        name="backward_part",
    )(*in_vmem(field), axial, sums, *in_vmem(lateral))


def finish_kernel(before, own, near, far, *refs, first, view_count):
    out, spread_out, turned, sem = refs[-4:]
    chunk, block_len, _ = before.shape
    spread = chunk + 1
    for i in range(chunk):
        total = own[i] + near[i] + far[i]
        spread_out[pl.ds(i, block_len, stride=spread), :] = before[i] * total / view_count
    copies = []
    for z in range(block_len):
        turned[z] = spread_out[pl.ds(z * spread, chunk), :]
        if (z + 1) % SENT == 0:
            part = pl.ds(z + 1 - SENT, SENT)
            target = out.at[part, pl.ds(first, chunk), :]
            copies.append(pltpu.make_async_copy(turned.at[part], target, sem.at[len(copies)]))
            copies[-1].start()
    for copy in copies:
        copy.wait()


def finish_part(before, own, near, far, result, first, size_x, view_count):
    chunk, block_len, size_y = before.shape
    vmem = pl.BlockSpec(memory_space=pltpu.VMEM)
    anywhere = pl.BlockSpec(memory_space=pl.ANY)
    extra = [] if result is None else [result]
    return pl.pallas_call(
        functools.partial(finish_kernel, first=first, view_count=view_count),
        in_specs=[vmem] * 4 + [anywhere] * len(extra),
        out_specs=anywhere,
        out_shape=jax.ShapeDtypeStruct((block_len, size_x, size_y), F32),
        scratch_shapes=[
            pltpu.VMEM((block_len * (chunk + 1), size_y), F32),
            pltpu.VMEM((block_len, chunk, size_y), F32),
            pltpu.SemaphoreType.DMA((block_len // SENT,)),
        ],
        input_output_aliases={4: 0} if extra else {},
        compiler_params=pltpu.CompilerParams(vmem_limit_bytes=VMEM_LIMIT),
        name="finish_part",
    )(*in_vmem(before, own, near, far), *extra)


def body(recorded, initial, kernel_x, kernel_y, kernel_z):
    view_count, block_len, size_x, size_y = recorded.shape
    assert kernel_z.shape[1] // 2 <= block_len
    count = lax.axis_size("slab")
    near_pairs = [p for i in range(0, count - 1, 2) for p in ((i, i + 1), (i + 1, i))]
    first_pairs = [p for i in range(3, count - 1, 4) for p in ((i, i + 1), (i + 1, i))]
    second_pairs = [p for i in range(1, count - 1, 4) for p in ((i, i + 1), (i + 1, i))]

    def swap(value, pairs):
        return lax.ppermute(value, "slab", pairs)

    planes = recorded.reshape(view_count * block_len, size_x, size_y)
    first = swap(initial, first_pairs)
    near = swap(initial, near_pairs)
    fwd_x, bwd_x, fwd_y, bwd_y, local_z, far_z, bwd_z, planes, sums = prepare(
        kernel_x, kernel_y, kernel_z, initial, planes, "slab"
    )
    delayed, sums = lax.optimization_barrier((initial, sums))
    sums = summed(sums, "slab")
    inner = [initial, near]
    far_halos = [first, swap(delayed, second_pairs)]
    chunk = size_x // CHUNKS
    far_pairs = first_pairs + second_pairs
    result = None
    for iteration in range(ITERS):
        last = iteration == ITERS - 1
        local = local_part(inner, local_z, block_len, size_x, not iteration)
        part = forward_part(far_halos, local, far_z, fwd_y, block_len, size_x, not iteration)
        field = quotient_part([part], planes, fwd_x, bwd_x)
        estimate, near_halos, far_halos = [], [], []
        sent = []
        for i in range(CHUNKS):
            sent.append(backward_part(field, bwd_z, sums, bwd_y, block_len, chunk, i * chunk))
        fars = [swap(far, far_pairs) for _, _, far in sent]
        nears = [swap(near, near_pairs) for _, near, _ in sent]
        for i, ((own, _, _), near, far) in enumerate(zip(sent, nears, fars)):
            rows = slice(i * chunk, (i + 1) * chunk)
            if last:
                result = finish_part(inner[i], own, near, far, result, i * chunk, size_x, view_count)
                continue
            if i:
                estimate[-1], far = lax.optimization_barrier((estimate[-1], far))
            before = inner[i] if iteration else jnp.transpose(initial[:, rows], (1, 0, 2))
            estimate.append(before * (own + near + far) / view_count)
            near_halos.append(swap(estimate[i], near_pairs))
            far_halos.append(swap(estimate[i], far_pairs))
        inner = estimate + near_halos
    return result


def solution(mesh):
    in_specs = (P(None, "slab", "groups", None), P("slab", "groups", None), P(), P(), P())
    out_specs = P("slab", "groups", None)
    return jax.shard_map(body, mesh=mesh, in_specs=in_specs, out_specs=out_specs, check_vma=False)
```

```python
import functools

import jax
import jax.numpy as jnp
from jax import lax
from jax.experimental import pallas as pl
from jax.experimental.pallas import tpu as pltpu
from jax.sharding import PartitionSpec as P


ITERS = 2
GROUP = 8
SENT = 4
CHUNKS = 2
VMEM_LIMIT = 16 << 20
ROWS = 64
ALONG_Y = 1
FORWARD_Z = 8
BACKWARD_Z = 8
DIVIDE = 8
BACK = 8
LANES = 128
F32 = jnp.float32
BF16 = jnp.bfloat16
PRECISE = lax.Precision.HIGHEST


def split(value):
    high = value.astype(BF16)
    low = (value - high.astype(F32)).astype(BF16)
    return high, low


def dot(left, right):
    return jnp.dot(left, right, preferred_element_type=F32)


def normalized_lines(taps, width):
    view_count, tap_count = taps.shape
    values = jnp.concatenate([taps[...], jnp.zeros((view_count, width - tap_count), F32)], axis=1)
    return values / jnp.sum(values, axis=1, keepdims=True)


def prepare_kernel(
    position, taken_x, taken_y, taken_z, initial_in, recorded_in,
    fwd_x, bwd_x, fwd_y, bwd_y, local_z, far_z, bwd_z, recorded, out,
    taps_x, taps_y, taps_z, initial, sems, *, count,
):
    view_count, tap_count = taps_x.shape
    block_len = initial.shape[0]
    pairs = [(taken_x, taps_x), (taken_y, taps_y), (taken_z, taps_z), (initial_in, initial)]
    for view in range(view_count):
        part = pl.ds(view * block_len, block_len)
        pairs.append((recorded_in.at[part], recorded.at[part]))
    copies = [pltpu.make_async_copy(*pair, sems.at[i]) for i, pair in enumerate(pairs)]
    for copy in copies:
        copy.start()
    for copy in copies[:3]:
        copy.wait()
    sums_x, sums_y, sums_z = [], [], []
    size = fwd_x.shape[1]
    rows = lax.broadcasted_iota(jnp.int32, (size, size), 0)
    cols = lax.broadcasted_iota(jnp.int32, (size, size), 1)
    tap_ids = cols - rows + tap_count // 2
    inside = (tap_ids >= 0) & (tap_ids < tap_count)
    for taps, is_x in ((taps_x, True), (taps_y, False)):
        values = normalized_lines(taps, size)
        for view in range(view_count):
            line = jnp.broadcast_to(values[view : view + 1, :], (size, size))
            matrix = pltpu.roll(line, size - tap_count // 2, 1, stride=1, stride_axis=0)
            matrix = jnp.where(inside, matrix, 0.0)
            high, low = split(matrix)
            high_t, low_t = split(matrix.T)
            total = jnp.sum(matrix, axis=0, keepdims=True)
            if is_x:
                fwd_x[view] = jnp.concatenate([high, high, low], axis=1)
                bwd_x[view] = jnp.concatenate([high_t, high_t, low_t], axis=1)
                sums_x.append(total)
            else:
                one = jnp.concatenate([high_t, low_t], axis=1)
                fwd_y[view] = jnp.concatenate([one, one], axis=0)
                one = jnp.concatenate([high, low], axis=1)
                bwd_y[view] = jnp.concatenate([one, one], axis=0)
                sums_y.append(total)

    planes = view_count * block_len
    reach = taps_z.shape[1] // 2
    place = position[0]
    odd = (place & 1) == 1
    rows = lax.broadcasted_iota(jnp.int32, (block_len, size), 0)
    cols = lax.broadcasted_iota(jnp.int32, (block_len, size), 1)
    target = place * block_len + rows + reach - cols
    kept = (target >= 0) & (target < count * block_len)
    values = normalized_lines(taps_z, size)
    bands = []
    for view in range(view_count):
        line = jnp.broadcast_to(values[view : view + 1, :], (block_len, size))
        total = jnp.sum(jnp.where(kept, line, 0.0), axis=1, keepdims=True)
        sums_z.append(jnp.broadcast_to(total, (block_len, size)))

        def moved(ahead):
            return pltpu.roll(line, (-ahead) % size, 1, stride=1, stride_axis=0)

        near = jnp.where(odd, moved(reach - 2 * block_len), moved(reach))
        far = jnp.where(odd, moved(reach - block_len), moved(reach - 3 * block_len))
        band = jnp.where(cols < block_len, moved(reach), jnp.where(cols < 2 * block_len, near, far))
        bands.append(jnp.where(cols < 3 * block_len, band, 0.0))
    matrix = jnp.concatenate(bands, axis=0)
    square = jnp.concatenate([matrix, jnp.zeros((size - planes, size), F32)], axis=0)
    blank = jnp.zeros((planes, size), F32)

    def spread(step, one, two, three):
        wide = [jnp.concatenate([value, blank], axis=1) for value in (one, two, three)]
        return wide[0] + pltpu.roll(wide[1], step, 1) + pltpu.roll(wide[2], 2 * step, 1)

    lanes = lax.broadcasted_iota(jnp.int32, matrix.shape, 1)
    ahead = pltpu.roll(matrix, size - 2 * block_len, 1)
    for ref, value, width in ((local_z, matrix, 2 * block_len), (far_z, ahead, block_len)):
        high, low = split(jnp.where(lanes < width, value, 0.0))
        high = high.astype(F32)
        ref[...] = spread(width, high, high, low.astype(F32)).astype(BF16)
    matrix = square.T[:planes]
    bwd_z[...] = spread(planes, matrix, matrix, matrix)

    copies[3].wait()
    flats = [jnp.zeros((size, LANES), F32) for _ in range(view_count)]
    for z in range(block_len):
        plane = initial[z]
        flats = [flat + plane * sums_z[view][z : z + 1, :] for view, flat in enumerate(flats)]
    lanes = lax.broadcasted_iota(jnp.int32, out.shape, 1)
    view_of = (lanes % planes) // block_len
    row_of = lax.broadcasted_iota(jnp.int32, out.shape, 0)
    result = jnp.zeros(out.shape, F32)
    for view in range(view_count):
        along_x = jnp.broadcast_to(sums_x[view], (8, size))
        weighted = jnp.dot(along_x, flats[view], precision=PRECISE, preferred_element_type=F32)
        blur_total = jnp.sum(weighted[:1] * sums_y[view])
        copies[4 + view].wait()

        def add(z, total):
            return total + jnp.sum(recorded[view * block_len + z].reshape(-1, 8, LANES), axis=0)

        data_total = jnp.sum(lax.fori_loop(0, block_len, add, jnp.zeros((8, LANES), F32), unroll=4))
        value = jnp.where(row_of == 0, data_total, blur_total)
        result = jnp.where(view_of == view, value, result)
    out[...] = result


def prepare(kernel_x, kernel_y, kernel_z, initial, recorded, axis):
    view_count, tap_count = kernel_x.shape
    block_len, size, size_y = initial.shape
    planes = view_count * block_len
    assert size == size_y == LANES and tap_count <= size and kernel_y.shape == kernel_x.shape
    assert view_count == 3 and 3 * block_len + kernel_z.shape[1] <= size
    anywhere = pl.BlockSpec(memory_space=pltpu.HBM)
    out = jax.ShapeDtypeStruct
    return pl.pallas_call(
        functools.partial(prepare_kernel, count=lax.axis_size(axis)),
        in_specs=[pl.BlockSpec(memory_space=pltpu.SMEM)] + [anywhere] * 5,
        out_shape=(
            out((view_count, size, 3 * size), BF16),
            out((view_count, size, 3 * size), BF16),
            pltpu.VMEM((view_count, 2 * size, 2 * size), BF16),
            out((view_count, 2 * size, 2 * size), BF16),
            out((planes, 2 * size), BF16),
            out((planes, 2 * size), BF16),
            out((planes, 2 * size), F32),
            pltpu.VMEM(recorded.shape, F32),
            out((8, 2 * LANES), F32),
        ),
        scratch_shapes=[
            *(pltpu.VMEM(taps.shape, F32) for taps in (kernel_x, kernel_y, kernel_z)),
            pltpu.VMEM(initial.shape, F32),
            pltpu.SemaphoreType.DMA((4 + view_count,)),
        ],
        compiler_params=pltpu.CompilerParams(vmem_limit_bytes=VMEM_LIMIT),
        name="prepare",
    )(
        lax.axis_index(axis).astype(jnp.int32).reshape(1),
        *(
            pltpu.with_memory_space_constraint(value, pltpu.HBM)
            for value in (kernel_x, kernel_y, kernel_z, initial, recorded)
        ),
    )


def summed(value, axis):
    count = lax.axis_size(axis)
    if count & (count - 1):
        return lax.psum(value, axis)
    steps = [1 << bit for bit in range(count.bit_length() - 1)]
    rounds = [[step] for step in steps[:2]]
    for step in steps[2::2]:
        rounds.append([step, 2 * step, 3 * step] if 2 * step < count else [step])
    for offsets in rounds:
        received = []
        for step in offsets:
            received.append(lax.ppermute(value, axis, [(i, i ^ step) for i in range(count)]))
        value = sum(received, value)
    return value


def in_vmem(*values):
    return [pltpu.with_memory_space_constraint(value, pltpu.VMEM) for value in values]


def windows(groups, scratch, turned):
    if not turned:
        chunk = groups[0][0].shape[0]

        def read(start, number):
            local = pl.ds(start - number * chunk, GROUP)
            return jnp.concatenate([group[number][local] for group in groups], axis=1)

        return read
    block_len, size_x, _ = groups[0][0].shape
    spread = size_x + 1
    for place, group in enumerate(groups):
        for z in range(block_len):
            plane = sum(ref[z] for ref in group)
            scratch[pl.ds((place * block_len + z) * spread, size_x), :] = plane
    depth = len(groups) * block_len

    def read_turned(start, number):
        return jnp.stack([scratch[pl.ds(start + i, depth, stride=spread), :] for i in range(GROUP)])

    return read_turned


def by_groups(body, size_x, unroll):
    steps = size_x // GROUP // CHUNKS
    for number in range(CHUNKS):
        lax.fori_loop(
            number * steps, (number + 1) * steps, functools.partial(body, number=number), 0, unroll=unroll
        )


def axial_terms(values):
    high, low = split(values)
    return jnp.concatenate([high, low, high], axis=1)


def local_kernel(*refs, turned):
    *parts, axial, out = refs[:-1] if turned else refs
    half = len(parts) // 2
    read = windows((parts[:half], parts[half:]), refs[-1], turned)
    size_x = out.shape[0]
    depth = parts[0].shape[0 if turned else 1]
    matrix = axial[:, : 6 * depth]

    def along_z(index, carry, number):
        start = index * GROUP
        terms = axial_terms(read(start, number))
        for pair in range(0, GROUP, 2):
            result = dot(matrix, jnp.concatenate([terms[pair], terms[pair + 1]], axis=1))
            out[start + pair] = result[:, :LANES]
            out[start + pair + 1] = result[:, LANES:]
        return carry

    by_groups(along_z, size_x, FORWARD_Z)


def local_part(parts, axial, block_len, size_x, turned):
    size_y = parts[0].shape[2]
    return pl.pallas_call(
        functools.partial(local_kernel, turned=turned),
        out_shape=pltpu.VMEM((size_x, axial.shape[0], size_y), F32),
        scratch_shapes=[pltpu.VMEM((2 * block_len * (size_x + 1), size_y), F32)] * turned,
        compiler_params=pltpu.CompilerParams(vmem_limit_bytes=VMEM_LIMIT),
        name="local_part",
    )(*in_vmem(*parts), axial)


def forward_kernel(*refs, block_len, turned):
    scratch = refs[-1]
    *fars, local, axial, lateral, out, fields = refs[:-1] if turned else refs
    size_x = local.shape[0]
    view_count = lateral.shape[0]
    matrix = axial[:, : 3 * block_len]
    spread = size_x + 1
    read = windows((fars,), scratch, turned)

    def along_z(index, carry, number):
        start = index * GROUP
        terms = axial_terms(read(start, number))
        for pair in range(0, GROUP, 2):
            result = dot(matrix, jnp.concatenate([terms[pair], terms[pair + 1]], axis=1))
            for side in (0, 1):
                row = (start + pair + side) * block_len
                mine = result[:, side * LANES : (side + 1) * LANES] + local[start + pair + side]
                high, low = split(mine)
                for view in range(view_count):
                    part = slice(view * block_len, (view + 1) * block_len)
                    fields[view, pl.ds(row, block_len), :LANES] = high[part]
                    fields[view, pl.ds(row, block_len), LANES:] = low[part]
        return carry

    by_groups(along_z, size_x, FORWARD_Z)

    def along_y(index, carry):
        start = index * ROWS
        for view in range(view_count):
            result = dot(fields[view, pl.ds(start * block_len, ROWS * block_len), :], lateral[view])
            result = result[:, :LANES] + result[:, LANES:]
            for i in range(ROWS):
                first = view * block_len * spread + start + i
                out[pl.ds(first, block_len, stride=spread), :] = result[
                    i * block_len : (i + 1) * block_len
                ]
        return carry

    lax.fori_loop(0, size_x // ROWS, along_y, 0, unroll=ALONG_Y)


def forward_part(fars, local, axial, lateral, block_len, size_x, turned):
    size_y = local.shape[2]
    view_count = lateral.shape[0]
    scratch = [pltpu.VMEM((view_count, size_x * block_len, 2 * size_y), BF16)]
    if turned:
        scratch.append(pltpu.VMEM((block_len * (size_x + 1), size_y), F32))
    return pl.pallas_call(
        functools.partial(forward_kernel, block_len=block_len, turned=turned),
        out_shape=pltpu.VMEM((view_count * block_len * (size_x + 1), size_y), F32),
        scratch_shapes=scratch,
        compiler_params=pltpu.CompilerParams(vmem_limit_bytes=VMEM_LIMIT),
        name="forward_part",
    )(*in_vmem(*fars, local), axial, *in_vmem(lateral))


def quotient_kernel(*refs, chunks, block_len):
    parts, (recorded, fwd, bwd, out, terms) = refs[:chunks], refs[chunks:]
    view_count = fwd.shape[0]
    planes = view_count * block_len
    size_x = fwd.shape[1]
    chunk = size_x // chunks
    spread = planes + 1

    for view in range(view_count):

        def divide(index, carry):
            plane = view * block_len + 2 * index
            field = jnp.concatenate(
                [
                    jnp.concatenate(
                        [ref[pl.ds((plane + side) * (chunk + 1), chunk), :] for ref in parts], axis=0
                    )
                    for side in (0, 1)
                ],
                axis=1,
            )
            high, low = split(field)
            blurred = dot(fwd[view], jnp.concatenate([high, low, high], axis=0))
            data = jnp.concatenate([recorded[plane], recorded[plane + 1]], axis=1)
            high, low = split(data / blurred)
            terms[index, :size_x] = high
            terms[index, size_x:] = low
            return carry

        lax.fori_loop(0, block_len // 2, divide, 0, unroll=DIVIDE)

        def back(index, carry):
            plane = view * block_len + 2 * index
            both = terms[index]
            result = dot(bwd[view], jnp.concatenate([both, both[:size_x]], axis=0))
            out[pl.ds(plane, size_x, stride=spread), :] = result[:, :LANES]
            out[pl.ds(plane + 1, size_x, stride=spread), :] = result[:, LANES:]
            return carry

        lax.fori_loop(0, block_len // 2, back, 0, unroll=BACK)


def quotient_part(parts, recorded, fwd, bwd):
    planes, size_x, size_y = recorded.shape
    view_count = fwd.shape[0]
    return pl.pallas_call(
        functools.partial(quotient_kernel, chunks=len(parts), block_len=planes // view_count),
        out_shape=pltpu.VMEM((size_x * (planes + 1), size_y), F32),
        scratch_shapes=[pltpu.VMEM((planes // view_count // 2, 2 * size_x, 2 * size_y), BF16)],
        compiler_params=pltpu.CompilerParams(vmem_limit_bytes=VMEM_LIMIT),
        name="quotient_part",
    )(*in_vmem(*parts, recorded, fwd, bwd))


def backward_kernel(field, axial, sums, lateral, own, near, far, terms, *, block_len, offset):
    chunk = own.shape[0]
    view_count = lateral.shape[0]
    planes = view_count * block_len
    spread = planes + 1
    scaled = (axial[...] * (sums[1:2, :] / sums[0:1, :]))[:, : 3 * planes]
    high, low = split(scaled)
    lanes = lax.broadcasted_iota(jnp.int32, scaled.shape, 1)
    axial_matrix = jnp.where(lanes < 2 * planes, high.astype(F32), low.astype(F32)).astype(BF16)

    def along_y(index, carry):
        start = index * ROWS
        for view in range(view_count):
            rows = jnp.concatenate(
                [
                    field[pl.ds((offset + start + i) * spread + view * block_len, block_len), :]
                    for i in range(ROWS)
                ],
                axis=0,
            )
            result = dot(jnp.concatenate(split(rows), axis=1), lateral[view])
            result = result[:, :LANES] + result[:, LANES:]
            high, low = split(result.reshape(ROWS, block_len, LANES))
            for place, part in enumerate((high, low, high)):
                row = place * planes + view * block_len
                terms[pl.ds(start, ROWS), row : row + block_len, :] = part
        return carry

    lax.fori_loop(0, chunk // ROWS, along_y, 0, unroll=ALONG_Y)

    def along_z(index, carry):
        start = index * GROUP
        for pair in range(0, GROUP, 2):
            both = jnp.concatenate([terms[start + pair], terms[start + pair + 1]], axis=1)
            sent = dot(axial_matrix, both)
            for side in (0, 1):
                lanes_of = slice(side * LANES, (side + 1) * LANES)
                for place, ref in enumerate((own, near, far)):
                    ref[start + pair + side] = sent[place * block_len : (place + 1) * block_len, lanes_of]
        return carry

    lax.fori_loop(0, chunk // GROUP, along_z, 0, unroll=BACKWARD_Z)


def backward_part(field, axial, sums, lateral, block_len, chunk, offset):
    size_y = field.shape[1]
    planes = lateral.shape[0] * block_len
    shape = pltpu.VMEM((chunk, block_len, size_y), F32)
    return pl.pallas_call(
        functools.partial(backward_kernel, block_len=block_len, offset=offset),
        out_shape=(shape,) * 3,
        scratch_shapes=[pltpu.VMEM((chunk, 3 * planes, size_y), BF16)],
        compiler_params=pltpu.CompilerParams(vmem_limit_bytes=VMEM_LIMIT),
        name="backward_part",
    )(*in_vmem(field), axial, sums, *in_vmem(lateral))


def finish_kernel(before, own, near, far, *refs, first, view_count):
    out, spread_out, turned, sem = refs[-4:]
    chunk, block_len, _ = before.shape
    spread = chunk + 1
    for i in range(chunk):
        total = own[i] + near[i] + far[i]
        spread_out[pl.ds(i, block_len, stride=spread), :] = before[i] * total / view_count
    copies = []
    for z in range(block_len):
        turned[z] = spread_out[pl.ds(z * spread, chunk), :]
        if (z + 1) % SENT == 0:
            part = pl.ds(z + 1 - SENT, SENT)
            target = out.at[part, pl.ds(first, chunk), :]
            copies.append(pltpu.make_async_copy(turned.at[part], target, sem.at[len(copies)]))
            copies[-1].start()
    for copy in copies:
        copy.wait()


def finish_part(before, own, near, far, result, first, size_x, view_count):
    chunk, block_len, size_y = before.shape
    vmem = pl.BlockSpec(memory_space=pltpu.VMEM)
    anywhere = pl.BlockSpec(memory_space=pl.ANY)
    extra = [] if result is None else [result]
    return pl.pallas_call(
        functools.partial(finish_kernel, first=first, view_count=view_count),
        in_specs=[vmem] * 4 + [anywhere] * len(extra),
        out_specs=anywhere,
        out_shape=jax.ShapeDtypeStruct((block_len, size_x, size_y), F32),
        scratch_shapes=[
            pltpu.VMEM((block_len * (chunk + 1), size_y), F32),
            pltpu.VMEM((block_len, chunk, size_y), F32),
            pltpu.SemaphoreType.DMA((block_len // SENT,)),
        ],
        input_output_aliases={4: 0} if extra else {},
        compiler_params=pltpu.CompilerParams(vmem_limit_bytes=VMEM_LIMIT),
        name="finish_part",
    )(*in_vmem(before, own, near, far), *extra)


def body(recorded, initial, kernel_x, kernel_y, kernel_z):
    view_count, block_len, size_x, size_y = recorded.shape
    assert kernel_z.shape[1] // 2 <= block_len
    count = lax.axis_size("slab")
    near_pairs = [p for i in range(0, count - 1, 2) for p in ((i, i + 1), (i + 1, i))]
    first_pairs = [p for i in range(3, count - 1, 4) for p in ((i, i + 1), (i + 1, i))]
    second_pairs = [p for i in range(1, count - 1, 4) for p in ((i, i + 1), (i + 1, i))]

    def swap(value, pairs):
        return lax.ppermute(value, "slab", pairs)

    planes = recorded.reshape(view_count * block_len, size_x, size_y)
    first = swap(initial, first_pairs)
    near = swap(initial, near_pairs)
    fwd_x, bwd_x, fwd_y, bwd_y, local_z, far_z, bwd_z, planes, sums = prepare(
        kernel_x, kernel_y, kernel_z, initial, planes, "slab"
    )
    delayed, sums = lax.optimization_barrier((initial, sums))
    sums = summed(sums, "slab")
    inner = [initial, near]
    far_halos = [first, swap(delayed, second_pairs)]
    chunk = size_x // CHUNKS
    far_pairs = first_pairs + second_pairs
    result = None
    for iteration in range(ITERS):
        last = iteration == ITERS - 1
        local = local_part(inner, local_z, block_len, size_x, not iteration)
        part = forward_part(far_halos, local, far_z, fwd_y, block_len, size_x, not iteration)
        field = quotient_part([part], planes, fwd_x, bwd_x)
        estimate, near_halos, far_halos = [], [], []
        sent = []
        for i in range(CHUNKS):
            sent.append(backward_part(field, bwd_z, sums, bwd_y, block_len, chunk, i * chunk))
        fars = [swap(far, far_pairs) for _, _, far in sent]
        nears = [swap(near, near_pairs) for _, near, _ in sent]
        for i, ((own, _, _), near, far) in enumerate(zip(sent, nears, fars)):
            rows = slice(i * chunk, (i + 1) * chunk)
            if last:
                result = finish_part(inner[i], own, near, far, result, i * chunk, size_x, view_count)
                continue
            if i:
                estimate[-1], far = lax.optimization_barrier((estimate[-1], far))
            before = inner[i] if iteration else jnp.transpose(initial[:, rows], (1, 0, 2))
            estimate.append(before * (own + near + far) / view_count)
            near_halos.append(swap(estimate[i], near_pairs))
            far_halos.append(swap(estimate[i], far_pairs))
        inner = estimate + near_halos
    return result


def solution(mesh):
    in_specs = (P(None, "slab", "groups", None), P("slab", "groups", None), P(), P(), P())
    out_specs = P("slab", "groups", None)
    return jax.shard_map(body, mesh=mesh, in_specs=in_specs, out_specs=out_specs, check_vma=False)
```
